256 devices in a mesh: dp: 32 (over z, x_lo, core), seq: 8 (over y, x_hi).
Axes of the slice: x: 4 (x_hi: 2, x_lo: 2; x = x_hi * 2 + x_lo), y: 4, z: 8, core: 2. Of those that a mesh axis runs over, the one named last changes fastest.
Arguments:
- inputs: bfloat16 [32, 1024, 1536], P('dp', 'seq'), may hold values from -45 to 45
- dilated_tap_weight: bfloat16 [3, 768, 1536], P(None, 'seq'), may hold values from -0.09375 to 0.09375
- point_weight: bfloat16 [768, 1536], P('seq'), may hold values from -0.21875 to 0.21875
- query_weight: bfloat16 [1536, 1536], P('seq'), may hold values from -0.21875 to 0.21875
- key_weight: bfloat16 [1536, 1536], P('seq'), may hold values from -0.21875 to 0.21875
- value_weight: bfloat16 [1536, 1536], P('seq'), may hold values from -0.15625 to 0.15625
- out_weight: bfloat16 [1536, 1536], P('seq'), may hold values from -0.4375 to 0.4375
- cotangent: bfloat16 [32, 1024, 1536], P('dp', 'seq'), may hold values from -6 to 6
Outputs:
- output: bfloat16 [32, 1024, 1536], P('dp', 'seq')
- dilated_tap_gradient: float32 [3, 1536, 768], P(None, 'dp', 'seq')
- point_grad: float32 [768, 1536], P('seq', 'dp')
- query_grad: float32 [1536, 1536], P('dp', 'seq')
- key_grad: float32 [1536, 1536], P('dp', 'seq')
- value_grad: float32 [1536, 1536], P('dp', 'seq')
- out_grad: float32 [1536, 1536], P('seq', 'dp')
The draws below stay inside these ranges and needn't reach their ends.
All inputs are finite; a program needn't handle non-finite values.
Results may differ from the reference program's by a relative error of at most 0.033.
Values may be sent and summed in bfloat16 or wider, within the bound.
A program may use at most 128 MiB of HBM per device.

```python
import math
import jax
import jax.numpy as jnp
from jax import lax

CH = 1536
MID = 768
HEADS = 8
HSIZE = 192
DILATION_STEP = 16
LEN = 1024
BATCH = 32
N_SEQ = 8


def draw_inputs(key, part):
    key_rows, key_cols, key_vals = jax.random.split(key, 3)
    row_scale = jnp.exp(jax.random.uniform(key_rows, (BATCH, LEN, 1), jnp.float32, -1.2, 1.1))
    col_scale = jnp.exp(jax.random.uniform(key_cols, (1, 1, CH), jnp.float32, -1.2, 1.1))
    value_rows = jnp.clip(jax.random.normal(key_vals, (BATCH, LEN, CH), jnp.float32), -5.0, 5.0)
    return (value_rows * row_scale * col_scale).astype(jnp.bfloat16)


def shard_levels(stream_key, shape, cuts, low, top_value):
    gain, own = 1.0, jax.random.fold_in(stream_key, 6)
    for dim, shards_of in cuts:
        heights = jnp.exp(jax.random.uniform(jax.random.fold_in(own, dim), (shards_of,), jnp.float32, low / len(cuts), top_value / len(cuts)))
        gain = gain * jnp.repeat(heights, shape[dim] // shards_of).reshape([-1 if axis == dim else 1 for axis in range(len(shape))])
    return gain


def normal_values(rng, shape, scale, reach, cuts=(), held_as=jnp.bfloat16):
    drawn = jax.random.normal(rng, shape, jnp.float32) * scale
    if len(cuts) > 0:
        drawn = shard_levels(rng, shape, cuts, -0.22, 0.18) * drawn
    return jnp.clip(drawn, min=-reach, max=reach).astype(held_as)


def setup_inputs(seed: int = 0) -> dict:
    keys = jax.random.split(jax.random.key(seed), 9)
    return {
        "inputs": draw_inputs(jax.random.fold_in(keys[8], 71), 0),
        "dilated_tap_weight": normal_values(keys[1], (3, MID, CH), (3 * CH) ** -0.5, 0.09375, ((1, 8),)),
        "point_weight": normal_values(keys[2], (MID, CH), MID ** -0.5, 0.21875, ((0, 8),)),
        "query_weight": normal_values(keys[3], (HEADS * HSIZE, CH), (CH // 2) ** -0.5, 0.21875, ((0, 8),)),
        "key_weight": normal_values(keys[4], (HEADS * HSIZE, CH), (CH // 2) ** -0.5, 0.21875, ((0, 8),)),
        "value_weight": normal_values(keys[5], (HEADS * HSIZE, CH), CH ** -0.5, 0.15625, ((0, 8),)),
        "out_weight": normal_values(keys[6], (HEADS * HSIZE, CH), (HEADS * HSIZE // 8) ** -0.5, 0.4375, ((0, 8),)),
        "cotangent": normal_values(keys[7], (BATCH, LEN, CH), 1.0, 6.0, ((0, 32), (1, 8))),
    }


EPSILON = 1e-06
SOFT_CAP = 6.0

def rms_scale(value_rows):
    return lax.rsqrt(lax.optimization_barrier(jnp.mean(value_rows * value_rows, axis=-1, keepdims=True)) + EPSILON)

def rows_shifted(value_rows, tap_shift):
    if tap_shift == 0:
        return value_rows
    padded_rows = jnp.pad(value_rows, ((DILATION_STEP, DILATION_STEP), (0, 0)))
    return padded_rows[DILATION_STEP + tap_shift:DILATION_STEP + tap_shift + value_rows.shape[0]]

def gelu_back(pre_act, upstream):
    return jax.vjp(jax.nn.gelu, pre_act)[1](upstream)[0]

def block_sum(pair_list):
    total = None
    for left_side, right_side in pair_list:
        length = left_side.shape[0]
        inner_len = left_side.shape[1] // N_SEQ
        left_blocks = left_side.reshape(length, N_SEQ, inner_len).astype(jnp.float32)
        right_blocks = right_side.reshape(N_SEQ, inner_len, right_side.shape[1]).astype(jnp.float32)
        partial_value = jnp.einsum('lsk,skc->slc', left_blocks, right_blocks)
        total = partial_value if total is None else total + partial_value
    rounded = lax.optimization_barrier(total.astype(jnp.bfloat16))
    return lax.optimization_barrier(jnp.sum(rounded.astype(jnp.float32), axis=0))

def split_heads(matrix):
    head_count = matrix.shape[1] // HSIZE
    return matrix.reshape(matrix.shape[0], head_count, HSIZE).transpose(1, 0, 2)

def join_heads(stacked):
    return stacked.transpose(1, 0, 2).reshape(stacked.shape[1], -1)

def head_pass(packed):
    query_h, key_h, value_h, dout_h = packed
    inv_root = 1.0 / math.sqrt(HSIZE)
    raw_score = jnp.dot(query_h, key_h.T, preferred_element_type=jnp.float32) * inv_root
    capped = SOFT_CAP * jnp.tanh(raw_score / SOFT_CAP)
    unnormed = jnp.exp(capped)
    soft_weights = unnormed / lax.optimization_barrier(jnp.sum(unnormed, axis=-1, keepdims=True))
    soft_low = soft_weights.astype(jnp.bfloat16)
    out_h = jnp.dot(soft_low, value_h, preferred_element_type=jnp.float32).astype(jnp.bfloat16)
    grad_soft = jnp.dot(dout_h, value_h.T, preferred_element_type=jnp.float32)
    grad_capped = soft_weights * (grad_soft - lax.optimization_barrier(jnp.sum(soft_weights * grad_soft, axis=-1, keepdims=True)))
    ratio = capped / SOFT_CAP
    grad_score = (grad_capped * (1.0 - ratio * ratio)).astype(jnp.bfloat16)
    grad_query = (jnp.dot(grad_score, key_h, preferred_element_type=jnp.float32) * inv_root).astype(jnp.bfloat16)
    grad_key = (jnp.dot(grad_score.T, query_h, preferred_element_type=jnp.float32) * inv_root).astype(jnp.bfloat16)
    grad_value = jnp.dot(soft_low.T, dout_h, preferred_element_type=jnp.float32).astype(jnp.bfloat16)
    return (out_h, grad_query, grad_key, grad_value)

def one_sequence(inputs, cotangent, dilated_tap_weight, point_weight, query_weight, key_weight, value_weight, out_weight):
    inv_tokens = 1.0 / math.sqrt(BATCH * LEN)
    input_full = inputs.astype(jnp.float32)
    gelu_output = jax.nn.gelu(input_full * rms_scale(input_full)).astype(jnp.bfloat16)
    convolution_preact = sum((jnp.dot(rows_shifted(gelu_output, (tap_position - 1) * DILATION_STEP), dilated_tap_weight[tap_position].T, preferred_element_type=jnp.float32) for tap_position in range(3)))
    middle = jax.nn.gelu(convolution_preact).astype(jnp.bfloat16)
    residual = (input_full + block_sum([(middle, point_weight)])).astype(jnp.bfloat16)
    residual_f32 = lax.optimization_barrier(residual).astype(jnp.float32)
    scale = rms_scale(residual_f32)
    normed = (residual_f32 * scale).astype(jnp.bfloat16)
    query_mat = jnp.dot(normed, query_weight.T, preferred_element_type=jnp.float32).astype(jnp.bfloat16)
    key_mat = jnp.dot(normed, key_weight.T, preferred_element_type=jnp.float32).astype(jnp.bfloat16)
    value_mat = jnp.dot(normed, value_weight.T, preferred_element_type=jnp.float32).astype(jnp.bfloat16)
    grad_y = (cotangent.astype(jnp.float32) * inv_tokens).astype(jnp.bfloat16)
    grad_heads = jnp.dot(grad_y, out_weight.T, preferred_element_type=jnp.float32).astype(jnp.bfloat16)
    results = lax.map(head_pass, (split_heads(query_mat), split_heads(key_mat), split_heads(value_mat), split_heads(grad_heads)))
    attended, query_delta, key_delta, value_delta = [join_heads(stacked) for stacked in results]
    output = (residual_f32 + block_sum([(attended, out_weight)])).astype(jnp.bfloat16)
    out_grad = jnp.dot(attended.T, grad_y, preferred_element_type=jnp.float32)
    query_grad = jnp.dot(normed.T, query_delta, preferred_element_type=jnp.float32)
    key_grad = jnp.dot(normed.T, key_delta, preferred_element_type=jnp.float32)
    value_grad = jnp.dot(normed.T, value_delta, preferred_element_type=jnp.float32)
    grad_normed = block_sum([(query_delta, query_weight), (key_delta, key_weight), (value_delta, value_weight)])
    grad_resid = (grad_y.astype(jnp.float32) + scale * grad_normed - residual_f32 * scale ** 3 * lax.optimization_barrier(jnp.mean(grad_normed * residual_f32, axis=-1, keepdims=True))).astype(jnp.bfloat16)
    grad_middle = jnp.dot(grad_resid, point_weight.T, preferred_element_type=jnp.float32)
    convolution_gradient = gelu_back(convolution_preact, grad_middle).astype(jnp.bfloat16)
    point_grad = jnp.dot(middle.T, grad_resid, preferred_element_type=jnp.float32)
    dilated_tap_gradient = jnp.stack([jnp.dot(rows_shifted(gelu_output, (tap_position - 1) * DILATION_STEP).T, convolution_gradient, preferred_element_type=jnp.float32) for tap_position in range(3)])
    return (output, dilated_tap_gradient, point_grad, query_grad, key_grad, value_grad, out_grad)

def reference(inputs, dilated_tap_weight, point_weight, query_weight, key_weight, value_weight, out_weight, cotangent):

    def scan_step(totals, sequence_pair):
        result = one_sequence(sequence_pair[0], sequence_pair[1], dilated_tap_weight, point_weight, query_weight, key_weight, value_weight, out_weight)
        new_totals = tuple((old + fresh for old, fresh in zip(totals, result[1:])))
        return (new_totals, result[0])
    zero_grads = (jnp.zeros((3, CH, MID), jnp.float32), jnp.zeros(point_weight.shape, jnp.float32), jnp.zeros((CH, HEADS * HSIZE), jnp.float32), jnp.zeros((CH, HEADS * HSIZE), jnp.float32), jnp.zeros((CH, HEADS * HSIZE), jnp.float32), jnp.zeros(out_weight.shape, jnp.float32))
    grad_sums, outputs = lax.scan(scan_step, zero_grads, (inputs, cotangent))
    return (outputs, grad_sums[0], grad_sums[1], grad_sums[2], grad_sums[3], grad_sums[4], grad_sums[5])
```

```python
import functools
import math

import jax
import jax.numpy as jnp
from jax import lax
from jax.experimental import pallas as pl
from jax.experimental.pallas import tpu as pltpu
from jax.sharding import Mesh
from jax.sharding import PartitionSpec as P

HSIZE = 192
STEP = 16
EPSILON = 1e-06
SOFT_CAP = 6.0
LEN = 1024
CH = 1536
INNER = 96
ROWS = 128
BATCH = 32
AXES = ("z", "xl", "c", "y", "xh")
DP = ("z", "xl", "c")
SEQ = ("y", "xh")
MESH_ID = pl.DeviceIdType.MESH
F32 = jnp.float32
BF16 = jnp.bfloat16
VMEM_SPEC = pl.BlockSpec(memory_space=pltpu.VMEM)
ANY_SPEC = pl.BlockSpec(memory_space=pl.ANY)
LIMIT = 62 * 1024 * 1024


def dot_nt(a, b):
    return lax.dot_general(a, b, (((1,), (1,)), ((), ())), preferred_element_type=F32)


def dot_nn(a, b):
    return jnp.dot(a, b, preferred_element_type=F32)


def dot_tn(a, b):
    return lax.dot_general(a, b, (((0,), (0,)), ((), ())), preferred_element_type=F32)


def rms_scale(rows):
    return lax.rsqrt(jnp.mean(rows * rows, axis=-1, keepdims=True) + EPSILON)


def gelu_back(pre_act, upstream):
    return jax.vjp(jax.nn.gelu, pre_act)[1](upstream)[0]


class Place:
    def __init__(self):
        self.z = lax.axis_index("z")
        self.xl = lax.axis_index("xl")
        self.c = lax.axis_index("c")
        self.y = lax.axis_index("y")
        self.xh = lax.axis_index("xh")
        self.up = {"y": lax.rem(self.y + 1, 4)}
        self.down = {"y": lax.rem(self.y + 3, 4)}
        self.twin = {"c": 1 - self.c}
        self.swap = {"xl": 1 - self.xl, "xh": self.c, "c": self.xh}

    def block(self, d, mine=True):
        return lax.rem(self.y + d, 4) * 2 + (self.c if mine else 1 - self.c)


def greet(devices):
    barrier = pltpu.get_barrier_semaphore()
    for device in devices:
        pl.semaphore_signal(barrier, inc=1, device_id=device, device_id_type=MESH_ID)
    pl.semaphore_wait(barrier, len(devices))


def remote(src, dst, send, recv, device):
    return pltpu.make_async_remote_copy(
        src_ref=src, dst_ref=dst, send_sem=send, recv_sem=recv,
        device_id=device, device_id_type=MESH_ID,
    )


class Gather:
    def __init__(self, place, view, send, recv):
        self.view, self.send, self.recv = view, send, recv
        p = place
        own, low, high, far = (p.block(d) for d in (0, 3, 1, 2))
        own2, low2, high2, far2 = (p.block(d, False) for d in (0, 3, 1, 2))
        self.out = [
            (own, 0, p.up), (own, 1, p.up), (low, 0, p.up),
            (own, 1, p.down), (own, 0, p.down), (high, 1, p.down),
            (own, None, p.twin), (low, None, p.twin), (high, None, p.twin), (far, None, p.twin),
        ]
        self.inn = [
            (low, 0), (low, 1), (far, 0), (high, 1), (high, 0), (far, 1),
            (own2, None), (low2, None), (high2, None), (far2, None),
        ]

    def copy(self, k):
        block, half, device = self.out[k]
        ref = self.view(block, half)
        return remote(ref, ref, self.send.at[k], self.recv.at[k], device)

    def start(self, *ks):
        for k in ks:
            self.copy(k).start()

    def arrive(self, *ks):
        for k in ks:
            block, half = self.inn[k]
            ref = self.view(block, half)
            remote(ref, ref, self.send.at[k], self.recv.at[k], self.out[k][2]).wait_recv()

    def begin(self):
        self.start(0, 3, 1, 4, 6)

    def forward(self):
        self.arrive(0)
        self.start(2)
        self.arrive(3)
        self.start(5)

    def share(self):
        self.arrive(1)
        self.start(7)
        self.arrive(4)
        self.start(8)

    def share_far(self):
        self.arrive(2, 5)
        self.start(9)

    def finish(self):
        for k in range(10):
            self.copy(k).wait_send()


def row_view(ref, pitch, rows):
    def view(block, half):
        if half is None:
            return ref.at[pl.ds(pl.multiple_of(block * pitch, pitch), rows)]
        start = pl.multiple_of(block * pitch + half * (rows // 2), 16)
        return ref.at[pl.ds(start, rows // 2)]
    return view


def column_view(ref):
    def view(block, half):
        columns = pl.ds(pl.multiple_of(block * 128, 128), 128)
        if half is None:
            return ref.at[:, columns]
        return ref.at[pl.ds(half * (LEN // 2), LEN // 2), columns]
    return view


def front_kernel(
    inv_tokens,
    x_ref, dil_ref, pw_ref, cot_ref, wq_ref, wk_ref, wv_ref, wo_ref,
    act, cpre, mid, resid_own, normed, q_o, k_o, v_o, gh_o, gy, wq, wk, wv, wo, pw_own,
    xall, taps, midall, pwall, cotall, dil,
    swap_send, swap_recv, ag_send, ag_recv,
):
    p = Place()
    mine = p.block(0)
    there = p.y * 2 + p.xh
    taps[0:STEP, :] = jnp.zeros((STEP, 384), F32)
    taps[LEN + STEP :, :] = jnp.zeros((STEP, 384), F32)
    for j in range(8):
        pwall[j * 128 + INNER : (j + 1) * 128, :] = jnp.zeros((32, CH), BF16)
    for k in range(3):
        dil[k * 128 + INNER : (k + 1) * 128, :] = jnp.zeros((32, CH), BF16)

    greet([p.swap, p.twin, p.up, p.down])

    def at(ref, block, pitch, rows):
        return ref.at[pl.ds(pl.multiple_of(block * pitch, pitch), rows)]

    swaps = [
        (x_ref.at[0], at(xall, there, ROWS, ROWS), at(xall, mine, ROWS, ROWS)),
        *[(dil_ref.at[k], dil.at[pl.ds(k * 128, INNER)], dil.at[pl.ds(k * 128, INNER)]) for k in range(3)],
        (pw_ref, at(pwall, there, 128, INNER), at(pwall, mine, 128, INNER)),
        (cot_ref.at[0], at(cotall, there, ROWS, ROWS), at(cotall, mine, ROWS, ROWS)),
        (wq_ref, wq, wq),
        (wk_ref, wk, wk),
        (wv_ref, wv, wv),
        (wo_ref, wo, wo),
    ]

    def swap_copy(k):
        src, dst, _ = swaps[k]
        return remote(src, dst, swap_send.at[k], swap_recv.at[k], p.swap)

    def swap_arrive(k):
        src, _, here = swaps[k]
        remote(src, here, swap_send.at[k], swap_recv.at[k], p.swap).wait_recv()

    for k in range(len(swaps)):
        swap_copy(k).start()

    ag_x = Gather(p, row_view(xall, ROWS, ROWS), ag_send.at[0], ag_recv.at[0])
    ag_pw = Gather(p, row_view(pwall, 128, INNER), ag_send.at[1], ag_recv.at[1])
    ag_mid = Gather(p, column_view(midall), ag_send.at[2], ag_recv.at[2])
    ag_cot = Gather(p, row_view(cotall, ROWS, ROWS), ag_send.at[3], ag_recv.at[3])

    def activate(d):
        base = lax.rem(p.y + d, 4) * 256

        @pl.loop(0, 8)
        def _(i):
            rows = pl.ds(pl.multiple_of(base + i * 32, 32), 32)
            value = xall[rows, :].astype(F32)
            act[rows, :] = jax.nn.gelu(value * rms_scale(value)).astype(BF16)

    def tap(d):
        base = pl.multiple_of(lax.rem(p.y + d, 4) * 256, 256)
        taps[pl.ds(base + STEP, 256), :] = dot_nt(act[pl.ds(base, 256), :], dil[...])

    swap_arrive(0)
    ag_x.begin()
    ag_x.arrive(6)
    activate(0)
    ag_x.forward()
    ag_x.share()
    for k in (1, 2, 3):
        swap_arrive(k)
    tap(0)
    ag_x.arrive(7)
    activate(3)
    tap(3)
    ag_x.share_far()
    swap_arrive(4)
    ag_pw.begin()
    ag_x.arrive(8)
    activate(1)
    tap(1)
    ag_pw.forward()
    ag_x.arrive(9)
    activate(2)
    tap(2)

    @pl.loop(0, 8)
    def _(i):
        base = pl.multiple_of(i * 128, 128)
        total = (
            taps[pl.ds(base, 128), 0:128]
            + taps[pl.ds(base + STEP, 128), 128:256]
            + taps[pl.ds(base + 2 * STEP, 128), 256:384]
        )
        cpre[pl.ds(base, 128), :] = total
        low = jax.nn.gelu(total).astype(BF16)
        mid[pl.ds(base, 128), :] = low
        midall[pl.ds(base, 128), pl.ds(pl.multiple_of(mine * 128, 128), 128)] = low

    ag_mid.begin()
    ag_pw.share()
    ag_pw.share_far()
    ag_mid.forward()
    swap_arrive(5)
    ag_cot.begin()
    ag_mid.share()
    ag_mid.share_far()
    ag_pw.arrive(6, 7, 8, 9)
    ag_cot.forward()
    ag_mid.arrive(6, 7, 8, 9)

    @pl.loop(0, 4)
    def _(i):
        rows = pl.ds(pl.multiple_of(i * 256, 256), 256)
        total = xall[rows, :].astype(F32) + dot_nn(midall[rows, :], pwall[...])
        low = total.astype(BF16)
        cotall_low = low.astype(F32)
        normed[rows, :] = (cotall_low * rms_scale(cotall_low)).astype(BF16)

        @pl.when(i == p.y)
        def _():
            half = pl.ds(pl.multiple_of(p.c * 128, 128), 128)
            act_rows = low
            resid_own[...] = jnp.where(p.c == 0, act_rows[0:128], act_rows[128:256])

    ag_cot.share()
    ag_cot.share_far()
    for k in (6, 7, 8):
        swap_arrive(k)

    @pl.loop(0, 4)
    def _(i):
        rows = pl.ds(pl.multiple_of(i * 256, 256), 256)
        tile = normed[rows, :]
        q_o[rows, :] = dot_nt(tile, wq[...]).astype(BF16)
        k_o[rows, :] = dot_nt(tile, wk[...]).astype(BF16)
        v_o[rows, :] = dot_nt(tile, wv[...]).astype(BF16)

    ag_cot.arrive(6, 7, 8, 9)
    swap_arrive(9)

    @pl.loop(0, 4)
    def _(i):
        rows = pl.ds(pl.multiple_of(i * 256, 256), 256)
        tile = (cotall[rows, :].astype(F32) * inv_tokens).astype(BF16)
        gy[rows, :] = tile
        gh_o[rows, :] = dot_nt(tile, wo[...]).astype(BF16)

    pw_own[...] = pwall[pl.ds(pl.multiple_of(mine * 128, 128), 128), :]
    for k in range(len(swaps)):
        swap_copy(k).wait_send()
    for ag in (ag_x, ag_pw, ag_mid, ag_cot):
        ag.finish()


def shape(*dims, dtype=BF16):
    return jax.ShapeDtypeStruct(dims, dtype)


def front(inv_tokens, x, dil, pw, cot, wq, wk, wv, wo):
    return pl.pallas_call(
        functools.partial(front_kernel, inv_tokens),
        name="front",
        out_shape=(
            shape(LEN, CH), shape(LEN, 128, dtype=F32), shape(LEN, 128), shape(ROWS, CH), shape(LEN, CH),
            *[shape(LEN, HSIZE)] * 4, shape(LEN, CH), *[shape(HSIZE, CH)] * 4, shape(128, CH),
        ),
        in_specs=[ANY_SPEC] * 8,
        out_specs=(VMEM_SPEC,) * 15,
        scratch_shapes=[
            pltpu.VMEM((LEN, CH), BF16),
            pltpu.VMEM((LEN + 2 * STEP, 384), F32),
            pltpu.VMEM((LEN, 1024), BF16),
            pltpu.VMEM((1024, CH), BF16),
            pltpu.VMEM((LEN, CH), BF16),
            pltpu.VMEM((384, CH), BF16),
            pltpu.SemaphoreType.DMA((10,)),
            pltpu.SemaphoreType.DMA((10,)),
            pltpu.SemaphoreType.DMA((4, 10)),
            pltpu.SemaphoreType.DMA((4, 10)),
        ],
        compiler_params=pltpu.CompilerParams(
            collective_id=0, has_side_effects=True, vmem_limit_bytes=LIMIT
        ),
    )(x, dil, pw, cot, wq, wk, wv, wo)


class Scatter:
    def __init__(self, place, part, near, made, land, send, recv):
        self.p, self.part, self.near, self.made, self.land = place, part, near, made, land
        self.send, self.recv = send, recv

    def own_rows(self, d, half):
        start = pl.multiple_of(self.p.block(d) * ROWS + half * 64, 64)
        return self.part[pl.ds(start, 64), :].astype(F32)

    def both(self, d, half):
        rows = slice(half * 64, half * 64 + 64)
        return self.own_rows(d, half) + self.near[d, rows, :].astype(F32)

    def copies(self, k):
        p = self.p
        if k < 4:
            start = pl.multiple_of(p.block(k, False) * ROWS, ROWS)
            return self.part.at[pl.ds(start, ROWS)], self.near.at[k], p.twin
        d, half, device = [
            (2, 0, p.down), (2, 1, p.up), (1, 0, p.up), (3, 1, p.down), (3, 0, p.down), (1, 1, p.up)
        ][k - 4]
        return self.made.at[k - 4], self.land.at[k - 4], device

    def copy(self, k):
        src, dst, device = self.copies(k)
        return remote(src, dst, self.send.at[k], self.recv.at[k], device)

    def begin(self):
        for d in (2, 1, 3, 0):
            self.copy(d).start()

    def make(self, k, value):
        self.made[k - 4, :, :] = value.astype(BF16)
        self.copy(k).start()

    def first(self):
        self.copy(2).wait_recv()
        self.make(4, self.both(2, 0))
        self.make(5, self.both(2, 1))
        self.copy(1).wait_recv()
        self.make(6, self.both(1, 0))
        self.copy(3).wait_recv()
        self.make(7, self.both(3, 1))

    def second(self):
        self.copy(4).wait_recv()
        self.make(8, self.both(3, 0) + self.land[0].astype(F32))
        self.copy(5).wait_recv()
        self.make(9, self.both(1, 1) + self.land[1].astype(F32))

    def total(self, out):
        self.copy(0).wait_recv()
        for k in (6, 7, 8, 9):
            self.copy(k).wait_recv()
        out[0:64, :] = self.both(0, 0) + self.land[2].astype(F32) + self.land[4].astype(F32)
        out[64:128, :] = self.both(0, 1) + self.land[3].astype(F32) + self.land[5].astype(F32)

    def finish(self):
        for k in range(10):
            self.copy(k).wait_send()


def sums_kernel(gn, op, gn_out, op_out, near, made, land, send, recv):
    p = Place()
    greet([p.twin, p.up, p.down])
    rs = [
        Scatter(p, part, near.at[k], made.at[k], land.at[k], send.at[k], recv.at[k])
        for k, part in enumerate((gn, op))
    ]
    rs[0].begin()
    rs[1].begin()
    rs[0].first()
    rs[0].second()
    rs[1].first()
    rs[0].total(gn_out)
    rs[1].second()
    rs[1].total(op_out)
    rs[0].finish()
    rs[1].finish()


def sums(gn, op):
    return pl.pallas_call(
        sums_kernel,
        name="sums",
        out_shape=(shape(ROWS, CH, dtype=F32),) * 2,
        in_specs=[VMEM_SPEC] * 2,
        out_specs=(VMEM_SPEC,) * 2,
        scratch_shapes=[
            pltpu.VMEM((2, 4, ROWS, CH), BF16),
            pltpu.VMEM((2, 6, 64, CH), BF16),
            pltpu.VMEM((2, 6, 64, CH), BF16),
            pltpu.SemaphoreType.DMA((2, 10)),
            pltpu.SemaphoreType.DMA((2, 10)),
        ],
        compiler_params=pltpu.CompilerParams(
            collective_id=1, has_side_effects=True, vmem_limit_bytes=LIMIT
        ),
    )(gn, op)


def spread_kernel(own_ref, out_ref, whole, back, send, recv, swap_send, swap_recv, local):
    p = Place()
    greet([p.twin, p.up, p.down])
    view = row_view(whole, ROWS, ROWS)
    load = pltpu.make_async_copy(own_ref, view(p.block(0), None), local)
    load.start()
    load.wait()
    ag = Gather(p, view, send, recv)
    ag.begin()
    ag.forward()
    ag.share()
    ag.share_far()
    ag.arrive(6, 7, 8, 9)
    out_ref[...] = whole[...]
    ag.finish()


def spread(own):
    return pl.pallas_call(
        spread_kernel,
        name="spread",
        out_shape=shape(LEN, CH),
        in_specs=[ANY_SPEC],
        out_specs=VMEM_SPEC,
        scratch_shapes=[
            pltpu.VMEM((LEN, CH), BF16),
            pltpu.VMEM((8, 128), BF16),
            pltpu.SemaphoreType.DMA((10,)),
            pltpu.SemaphoreType.DMA((10,)),
            pltpu.SemaphoreType.DMA((1,)),
            pltpu.SemaphoreType.DMA((1,)),
            pltpu.SemaphoreType.DMA,
        ],
        compiler_params=pltpu.CompilerParams(
            collective_id=2, has_side_effects=True, vmem_limit_bytes=LIMIT
        ),
    )(own)


class Reduce:
    def __init__(self, place, grad, r1a, r1b, sa, sb, r2a, r2b, quarter, landed, final, home, send, recv):
        self.p, self.grad = place, grad
        self.r1a, self.r1b, self.sa, self.sb, self.r2a, self.r2b = r1a, r1b, sa, sb, r2a, r2b
        self.quarter, self.landed, self.final, self.home = quarter, landed, final, home
        self.send, self.recv = send, recv
        p = place
        self.near = {"xl": 1 - p.xl}
        self.cross = {"xl": 1 - p.xl, "xh": 1 - p.xh}
        odd = lax.rem(p.xl + p.xh, 2)
        self.keep = [lax.rem(odd + 1 - k, 2) for k in range(2)]

    def copy(self, k):
        p = self.p
        if k < 2:
            src, dst, device = self.grad.at[pl.ds(0, 4), k, 1 - self.keep[k]], self.r1a.at[:, k], self.near
        elif k < 4:
            src, dst, device = self.grad.at[pl.ds(4, 4), k - 2, 1 - p.xh], self.r1b.at[:, k - 2], self.cross
        elif k == 4:
            src, dst, device = self.sa, self.r2a, self.cross
        elif k == 5:
            src, dst, device = self.sb, self.r2b, self.near
        elif k < 13:
            dz = k - 5
            target = lax.rem(p.z + dz, 8)
            src, dst, device = self.quarter.at[target], self.landed.at[dz - 1], {"z": target}
        else:
            src, dst, device = self.final, self.home, p.swap
        return remote(src, dst, self.send.at[k], self.recv.at[k], device)

    def begin(self):
        for k in range(4):
            self.copy(k).start()

    def pick_a(self, k):
        return self.grad[0:4, k, self.keep[k]].astype(F32) + self.r1a[:, k].astype(F32)

    def second(self):
        p = self.p
        for k in range(4):
            self.copy(k).wait_recv()
        keep = [self.grad[0:4, k, self.keep[k]].astype(F32) + self.r1a[:, k].astype(F32) for k in range(2)]
        mine = p.xl == 0
        self.sa[...] = jnp.where(mine, keep[0], keep[1]).astype(BF16)
        self.copy(4).start()
        self.quarter[0:4] = jnp.where(mine, keep[1], keep[0]).astype(BF16)
        keep = [self.grad[4:8, k, p.xh].astype(F32) + self.r1b[:, k].astype(F32) for k in range(2)]
        self.sb[...] = jnp.where(mine, keep[0], keep[1]).astype(BF16)
        self.copy(5).start()
        self.quarter[4:8] = jnp.where(mine, keep[1], keep[0]).astype(BF16)

    def third(self):
        self.copy(4).wait_recv()
        self.quarter[0:4] = (self.quarter[0:4].astype(F32) + self.r2a[...].astype(F32)).astype(BF16)
        self.copy(5).wait_recv()
        self.quarter[4:8] = (self.quarter[4:8].astype(F32) + self.r2b[...].astype(F32)).astype(BF16)
        for dz in (4, 3, 5, 2, 6, 1, 7):
            self.copy(5 + dz).start()

    def fourth(self):
        total = self.quarter[self.p.z].astype(F32)
        for dz in range(1, 8):
            self.copy(5 + dz).wait_recv()
            total = total + self.landed[dz - 1].astype(F32)
        self.final[...] = total.astype(BF16)
        self.copy(13).start()

    def finish(self):
        self.copy(13).wait_recv()
        for k in range(14):
            self.copy(k).wait_send()


def reduce_kernel(grad, home, r1a, r1b, sa, sb, r2a, r2b, quarter, landed, final, send, recv):
    p = Place()
    rd = Reduce(p, grad, r1a, r1b, sa, sb, r2a, r2b, quarter, landed, final, home, send, recv)
    greet([rd.near, rd.cross, p.swap, *[{"z": lax.rem(p.z + dz, 8)} for dz in range(1, 8)]])
    rd.begin()
    rd.second()
    rd.third()
    rd.fourth()
    rd.finish()


def reduce_batch(grad):
    width = grad.shape[-1]
    return pl.pallas_call(
        reduce_kernel,
        name="reduce",
        out_shape=shape(48, width),
        in_specs=[VMEM_SPEC],
        out_specs=VMEM_SPEC,
        scratch_shapes=[
            pltpu.VMEM((4, 2, 48, width), BF16),
            pltpu.VMEM((4, 2, 48, width), BF16),
            pltpu.VMEM((4, 48, width), BF16),
            pltpu.VMEM((4, 48, width), BF16),
            pltpu.VMEM((4, 48, width), BF16),
            pltpu.VMEM((4, 48, width), BF16),
            pltpu.VMEM((8, 48, width), BF16),
            pltpu.VMEM((7, 48, width), BF16),
            pltpu.VMEM((48, width), BF16),
            pltpu.SemaphoreType.DMA((14,)),
            pltpu.SemaphoreType.DMA((14,)),
        ],
        compiler_params=pltpu.CompilerParams(
            collective_id=3, has_side_effects=True, vmem_limit_bytes=LIMIT
        ),
    )(grad)


def head_pass(query_h, key_h, value_h, dout_h):
    inv_root = 1.0 / math.sqrt(HSIZE)
    raw_score = dot_nt(query_h, key_h) * inv_root
    capped = SOFT_CAP * jnp.tanh(raw_score / SOFT_CAP)
    unnormed = jnp.exp(capped)
    soft_weights = unnormed / jnp.sum(unnormed, axis=-1, keepdims=True)
    soft_low = soft_weights.astype(BF16)
    out_h = dot_nn(soft_low, value_h).astype(BF16)
    grad_soft = dot_nt(dout_h, value_h)
    grad_capped = soft_weights * (
        grad_soft - jnp.sum(soft_weights * grad_soft, axis=-1, keepdims=True)
    )
    ratio = capped / SOFT_CAP
    grad_score = (grad_capped * (1.0 - ratio * ratio)).astype(BF16)
    grad_query = (dot_nn(grad_score, key_h) * inv_root).astype(BF16)
    grad_key = (dot_tn(grad_score, query_h) * inv_root).astype(BF16)
    grad_value = dot_tn(soft_low, dout_h).astype(BF16)
    return (out_h, grad_query, grad_key, grad_value)


def rows_shifted(value_rows, tap_shift):
    padded_rows = jnp.pad(value_rows, ((STEP, STEP), (0, 0)))
    return padded_rows[STEP + tap_shift : STEP + tap_shift + value_rows.shape[0]]


def trade_pairs():
    pairs = []
    for xl in range(2):
        for c in range(2):
            for xh in range(2):
                pairs.append((xl * 4 + c * 2 + xh, (1 - xl) * 4 + xh * 2 + c))
    return pairs


def shards(x, dil, pw, wq, wk, wv, wo, cot):
    inv_tokens = 1.0 / math.sqrt(BATCH * LEN)
    (act, cpre, mid, resid, normed, q, k, v, gh, gy, wq, wk, wv, wo, pw) = front(
        inv_tokens, x, dil, pw, cot, wq, wk, wv, wo
    )
    attended, dq, dk, dv = head_pass(q, k, v, gh)
    gn_part = (dot_nn(dq, wq) + dot_nn(dk, wk) + dot_nn(dv, wv)).astype(BF16)
    op_part = dot_nn(attended, wo).astype(BF16)
    gn, op = sums(gn_part, op_part)
    resid_f32 = resid.astype(F32)
    output = (resid_f32 + op).astype(BF16)
    output = lax.ppermute(output, ("xl", "c", "xh"), trade_pairs())[None]
    own = lax.axis_index("y") * 2 + lax.axis_index("c")
    gy_own = lax.dynamic_slice_in_dim(gy, own * ROWS, ROWS, 0).astype(F32)
    scale = rms_scale(resid_f32)
    gr_own = (
        gy_own
        + scale * gn
        - resid_f32 * scale**3 * jnp.mean(gn * resid_f32, axis=-1, keepdims=True)
    ).astype(BF16)
    gr = spread(gr_own)
    gconv = gelu_back(cpre[:, :INNER], dot_nt(gr, pw[:INNER])).astype(BF16)
    moved = jnp.concatenate(
        [rows_shifted(gconv, STEP), gconv, rows_shifted(gconv, -STEP)], axis=1
    )
    grads = jnp.concatenate(
        [
            dot_tn(normed, jnp.concatenate([dq, dk, dv], axis=1)).astype(BF16),
            dot_tn(gy, attended).astype(BF16),
            dot_tn(act, moved).astype(BF16),
            dot_tn(gr, mid[:, :INNER]).astype(BF16),
        ],
        axis=1,
    )
    home = reduce_batch(grads.reshape(8, 2, 2, 48, grads.shape[1])).astype(F32)
    gq, gk, gv, go, gd, gp = jnp.split(home, [192, 384, 576, 768, 1056], axis=1)
    return (
        output,
        gd.reshape(48, 3, INNER).transpose(1, 0, 2),
        gp.T,
        gq,
        gk,
        gv,
        go.T,
    )


def solution(mesh):
    torus = Mesh(mesh.devices.reshape(8, 2, 2, 4, 2), AXES)
    in_specs = (
        P(DP, SEQ, None),
        P(None, SEQ, None),
        P(SEQ, None),
        P(SEQ, None),
        P(SEQ, None),
        P(SEQ, None),
        P(SEQ, None),
        P(DP, SEQ, None),
    )
    out_specs = (
        P(DP, SEQ, None),
        P(None, DP, SEQ),
        P(SEQ, DP),
        P(DP, SEQ),
        P(DP, SEQ),
        P(DP, SEQ),
        P(SEQ, DP),
    )
    return jax.shard_map(
        shards, mesh=torus, in_specs=in_specs, out_specs=out_specs, check_vma=False
    )
```

```python
import functools
import math

import jax
import jax.numpy as jnp
from jax import lax
from jax.experimental import pallas as pl
from jax.experimental.pallas import tpu as pltpu
from jax.sharding import Mesh
from jax.sharding import PartitionSpec as P

HSIZE = 192
STEP = 16
EPSILON = 1e-06
SOFT_CAP = 6.0
LEN = 1024
CH = 1536
INNER = 96
ROWS = 128
BATCH = 32
AXES = ("z", "xl", "c", "y", "xh")
DP = ("z", "xl", "c")
SEQ = ("y", "xh")
MESH_ID = pl.DeviceIdType.MESH
F32 = jnp.float32
BF16 = jnp.bfloat16
VMEM_SPEC = pl.BlockSpec(memory_space=pltpu.VMEM)
ANY_SPEC = pl.BlockSpec(memory_space=pl.ANY)
LIMIT = 62 * 1024 * 1024


def dot_nt(a, b):
    return lax.dot_general(a, b, (((1,), (1,)), ((), ())), preferred_element_type=F32)


def dot_nn(a, b):
    return jnp.dot(a, b, preferred_element_type=F32)


def dot_tn(a, b):
    return lax.dot_general(a, b, (((0,), (0,)), ((), ())), preferred_element_type=F32)


def rms_scale(rows):
    return lax.rsqrt(jnp.mean(rows * rows, axis=-1, keepdims=True) + EPSILON)


def gelu_back(pre_act, upstream):
    return jax.vjp(jax.nn.gelu, pre_act)[1](upstream)[0]


class Place:
    def __init__(self):
        self.z = lax.axis_index("z")
        self.xl = lax.axis_index("xl")
        self.c = lax.axis_index("c")
        self.y = lax.axis_index("y")
        self.xh = lax.axis_index("xh")
        self.up = {"y": lax.rem(self.y + 1, 4)}
        self.down = {"y": lax.rem(self.y + 3, 4)}
        self.twin = {"c": 1 - self.c}
        self.swap = {"xl": 1 - self.xl, "xh": self.c, "c": self.xh}

    def block(self, d, mine=True):
        return lax.rem(self.y + d, 4) * 2 + (self.c if mine else 1 - self.c)


def greet(devices):
    barrier = pltpu.get_barrier_semaphore()
    for device in devices:
        pl.semaphore_signal(barrier, inc=1, device_id=device, device_id_type=MESH_ID)
    pl.semaphore_wait(barrier, len(devices))


def remote(src, dst, send, recv, device):
    return pltpu.make_async_remote_copy(
        src_ref=src, dst_ref=dst, send_sem=send, recv_sem=recv,
        device_id=device, device_id_type=MESH_ID,
    )


class Gather:
    def __init__(self, place, view, send, recv):
        self.view, self.send, self.recv = view, send, recv
        p = place
        own, low, high, far = (p.block(d) for d in (0, 3, 1, 2))
        own2, low2, high2, far2 = (p.block(d, False) for d in (0, 3, 1, 2))
        self.out = [
            (own, 0, p.up), (own, 1, p.up), (low, 0, p.up),
            (own, 1, p.down), (own, 0, p.down), (high, 1, p.down),
            (own, None, p.twin), (low, None, p.twin), (high, None, p.twin), (far, None, p.twin),
        ]
        self.inn = [
            (low, 0), (low, 1), (far, 0), (high, 1), (high, 0), (far, 1),
            (own2, None), (low2, None), (high2, None), (far2, None),
        ]

    def copy(self, k):
        block, half, device = self.out[k]
        ref = self.view(block, half)
        return remote(ref, ref, self.send.at[k], self.recv.at[k], device)

    def start(self, *ks):
        for k in ks:
            self.copy(k).start()

    def arrive(self, *ks):
        for k in ks:
            block, half = self.inn[k]
            ref = self.view(block, half)
            remote(ref, ref, self.send.at[k], self.recv.at[k], self.out[k][2]).wait_recv()

    def begin(self):
        self.start(0, 3, 1, 4, 6)

    def forward(self):
        self.arrive(0)
        self.start(2)
        self.arrive(3)
        self.start(5)

    def share(self):
        self.arrive(1)
        self.start(7)
        self.arrive(4)
        self.start(8)

    def share_far(self):
        self.arrive(2, 5)
        self.start(9)

    def finish(self):
        for k in range(10):
            self.copy(k).wait_send()


def row_view(ref, pitch, rows):
    def view(block, half):
        if half is None:
            return ref.at[pl.ds(pl.multiple_of(block * pitch, pitch), rows)]
        start = pl.multiple_of(block * pitch + half * (rows // 2), 16)
        return ref.at[pl.ds(start, rows // 2)]
    return view


def column_view(ref):
    def view(block, half):
        columns = pl.ds(pl.multiple_of(block * 128, 128), 128)
        if half is None:
            return ref.at[:, columns]
        return ref.at[pl.ds(half * (LEN // 2), LEN // 2), columns]
    return view


class Scatter:
    def __init__(self, place, part, near, made, land, send, recv):
        self.p, self.part, self.near, self.made, self.land = place, part, near, made, land
        self.send, self.recv = send, recv

    def own_rows(self, d, half):
        start = pl.multiple_of(self.p.block(d) * ROWS + half * 64, 64)
        return self.part[pl.ds(start, 64), :].astype(F32)

    def both(self, d, half):
        rows = slice(half * 64, half * 64 + 64)
        return self.own_rows(d, half) + self.near[d, rows, :].astype(F32)

    def copies(self, k):
        p = self.p
        if k < 4:
            start = pl.multiple_of(p.block(k, False) * ROWS, ROWS)
            return self.part.at[pl.ds(start, ROWS)], self.near.at[k], p.twin
        d, half, device = [
            (2, 0, p.down), (2, 1, p.up), (1, 0, p.up), (3, 1, p.down), (3, 0, p.down), (1, 1, p.up)
        ][k - 4]
        return self.made.at[k - 4], self.land.at[k - 4], device

    def copy(self, k):
        src, dst, device = self.copies(k)
        return remote(src, dst, self.send.at[k], self.recv.at[k], device)

    def begin(self):
        for d in (2, 1, 3, 0):
            self.copy(d).start()

    def make(self, k, value):
        self.made[k - 4, :, :] = value.astype(BF16)
        self.copy(k).start()

    def first(self):
        self.copy(2).wait_recv()
        self.make(4, self.both(2, 0))
        self.make(5, self.both(2, 1))
        self.copy(1).wait_recv()
        self.make(6, self.both(1, 0))
        self.copy(3).wait_recv()
        self.make(7, self.both(3, 1))

    def second(self):
        self.copy(4).wait_recv()
        self.make(8, self.both(3, 0) + self.land[0].astype(F32))
        self.copy(5).wait_recv()
        self.make(9, self.both(1, 1) + self.land[1].astype(F32))

    def total(self, out):
        self.copy(0).wait_recv()
        for k in (6, 7, 8, 9):
            self.copy(k).wait_recv()
        out[0:64, :] = self.both(0, 0) + self.land[2].astype(F32) + self.land[4].astype(F32)
        out[64:128, :] = self.both(0, 1) + self.land[3].astype(F32) + self.land[5].astype(F32)

    def finish(self):
        for k in range(10):
            self.copy(k).wait_send()


class Reduce:
    def __init__(self, place, grad, r1a, r1b, sa, sb, r2a, r2b, quarter, landed, final, home, send, recv):
        self.p, self.grad = place, grad
        self.r1a, self.r1b, self.sa, self.sb, self.r2a, self.r2b = r1a, r1b, sa, sb, r2a, r2b
        self.quarter, self.landed, self.final, self.home = quarter, landed, final, home
        self.send, self.recv = send, recv
        p = place
        self.near = {"xl": 1 - p.xl}
        self.cross = {"xl": 1 - p.xl, "xh": 1 - p.xh}
        odd = lax.rem(p.xl + p.xh, 2)
        self.keep = [lax.rem(odd + 1 - k, 2) for k in range(2)]

    def copy(self, k):
        p = self.p
        if k < 2:
            src, dst, device = self.grad.at[pl.ds(0, 4), k, 1 - self.keep[k]], self.r1a.at[:, k], self.near
        elif k < 4:
            src, dst, device = self.grad.at[pl.ds(4, 4), k - 2, 1 - p.xh], self.r1b.at[:, k - 2], self.cross
        elif k == 4:
            src, dst, device = self.sa, self.r2a, self.cross
        elif k == 5:
            src, dst, device = self.sb, self.r2b, self.near
        elif k < 13:
            dz = k - 5
            target = lax.rem(p.z + dz, 8)
            src, dst, device = self.quarter.at[target], self.landed.at[dz - 1], {"z": target}
        else:
            src, dst, device = self.final, self.home, p.swap
        return remote(src, dst, self.send.at[k], self.recv.at[k], device)

    def begin(self):
        for k in range(4):
            self.copy(k).start()

    def second(self):
        p = self.p
        for k in range(4):
            self.copy(k).wait_recv()
        keep = [self.grad[0:4, k, self.keep[k]].astype(F32) + self.r1a[:, k].astype(F32) for k in range(2)]
        mine = p.xl == 0
        self.sa[...] = jnp.where(mine, keep[0], keep[1]).astype(BF16)
        self.copy(4).start()
        self.quarter[0:4] = jnp.where(mine, keep[1], keep[0]).astype(BF16)
        keep = [self.grad[4:8, k, p.xh].astype(F32) + self.r1b[:, k].astype(F32) for k in range(2)]
        self.sb[...] = jnp.where(mine, keep[0], keep[1]).astype(BF16)
        self.copy(5).start()
        self.quarter[4:8] = jnp.where(mine, keep[1], keep[0]).astype(BF16)

    def third(self):
        self.copy(4).wait_recv()
        self.quarter[0:4] = (self.quarter[0:4].astype(F32) + self.r2a[...].astype(F32)).astype(BF16)
        self.copy(5).wait_recv()
        self.quarter[4:8] = (self.quarter[4:8].astype(F32) + self.r2b[...].astype(F32)).astype(BF16)
        for dz in (4, 3, 5, 2, 6, 1, 7):
            self.copy(5 + dz).start()

    def fourth(self):
        total = self.quarter[self.p.z].astype(F32)
        for dz in range(1, 8):
            self.copy(5 + dz).wait_recv()
            total = total + self.landed[dz - 1].astype(F32)
        self.final[...] = total.astype(BF16)
        self.copy(13).start()

    def finish(self):
        self.copy(13).wait_recv()
        for k in range(14):
            self.copy(k).wait_send()


INV_ROOT = 1.0 / math.sqrt(HSIZE)


def layer_kernel(
    inv_tokens,
    x_ref, dil_ref, pw_ref, cot_ref, wq_ref, wk_ref, wv_ref, wo_ref,
    out_home, home1, home2,
    xall, act, taps, cpre, mid, midall, pwall, cotall, normed, dil, wqkv, wo, pw_own, resid,
    q_b, k_b, v_b, gh_b, att, dcat, dk_acc, dv_acc, gr, gpad, moved, rows_f32, out_low,
    near, made, land, red1, red2,
    swap_send, swap_recv, ag_send, ag_recv, rs_send, rs_recv, rd_send, rd_recv, home_send, home_recv,
):
    p = Place()
    mine = p.block(0)
    there = p.y * 2 + p.xh
    taps[0:STEP, :] = jnp.zeros((STEP, 384), F32)
    taps[LEN + STEP :, :] = jnp.zeros((STEP, 384), F32)
    gpad[0:STEP, :] = jnp.zeros((STEP, 128), BF16)
    gpad[LEN + STEP :, :] = jnp.zeros((STEP, 128), BF16)
    for j in range(8):
        pwall[j * 128 + INNER : (j + 1) * 128, :] = jnp.zeros((32, CH), BF16)
    for k in range(3):
        dil[k * 128 + INNER : (k + 1) * 128, :] = jnp.zeros((32, CH), BF16)

    rd1 = Reduce(p, *red1, home1, rd_send.at[0], rd_recv.at[0])
    rd2 = Reduce(p, *red2, home2, rd_send.at[1], rd_recv.at[1])
    greet(
        [p.swap, p.twin, p.up, p.down, rd1.near, rd1.cross]
        + [{"z": lax.rem(p.z + dz, 8)} for dz in range(1, 8)]
    )

    def at(ref, block, pitch, rows):
        return ref.at[pl.ds(pl.multiple_of(block * pitch, pitch), rows)]

    def piece(ref, k, rows):
        return ref.at[pl.ds(k, rows)]

    swaps = [
        (x_ref.at[0], at(xall, there, ROWS, ROWS), at(xall, mine, ROWS, ROWS)),
        *[(dil_ref.at[k], piece(dil, k * 128, INNER), piece(dil, k * 128, INNER)) for k in range(3)],
        (pw_ref, at(pwall, there, 128, INNER), at(pwall, mine, 128, INNER)),
        (cot_ref.at[0], at(cotall, there, ROWS, ROWS), at(cotall, mine, ROWS, ROWS)),
        (wq_ref, piece(wqkv, 0, HSIZE), piece(wqkv, 0, HSIZE)),
        (wk_ref, piece(wqkv, HSIZE, HSIZE), piece(wqkv, HSIZE, HSIZE)),
        (wv_ref, piece(wqkv, 2 * HSIZE, HSIZE), piece(wqkv, 2 * HSIZE, HSIZE)),
        (wo_ref, wo, wo),
    ]

    def swap_copy(k):
        src, dst, _ = swaps[k]
        return remote(src, dst, swap_send.at[k], swap_recv.at[k], p.swap)

    def swap_arrive(k):
        src, _, here = swaps[k]
        remote(src, here, swap_send.at[k], swap_recv.at[k], p.swap).wait_recv()

    for k in range(len(swaps)):
        swap_copy(k).start()

    ag_x = Gather(p, row_view(xall, ROWS, ROWS), ag_send.at[0], ag_recv.at[0])
    ag_pw = Gather(p, row_view(pwall, 128, INNER), ag_send.at[1], ag_recv.at[1])
    ag_mid = Gather(p, column_view(midall), ag_send.at[2], ag_recv.at[2])
    ag_cot = Gather(p, row_view(cotall, ROWS, ROWS), ag_send.at[3], ag_recv.at[3])
    ag_gr = Gather(p, row_view(gr, ROWS, ROWS), ag_send.at[4], ag_recv.at[4])

    def pair_rows(d):
        return pl.multiple_of(lax.rem(p.y + d, 4) * 256, 256)

    def activate(d):
        base = pair_rows(d)

        @pl.loop(0, 8)
        def _(i):
            rows = pl.ds(pl.multiple_of(base + i * 32, 32), 32)
            value = xall[rows, :].astype(F32)
            act[rows, :] = jax.nn.gelu(value * rms_scale(value)).astype(BF16)

    def tap(d):
        base = pair_rows(d)
        taps[pl.ds(base + STEP, 256), :] = dot_nt(act[pl.ds(base, 256), :], dil[...])

    swap_arrive(0)
    ag_x.begin()
    ag_x.arrive(6)
    activate(0)
    ag_x.forward()
    ag_x.share()
    for k in (1, 2, 3):
        swap_arrive(k)
    tap(0)
    ag_x.arrive(7)
    activate(3)
    tap(3)
    ag_x.share_far()
    swap_arrive(4)
    ag_pw.begin()
    ag_x.arrive(8)
    activate(1)
    tap(1)
    ag_pw.forward()
    ag_x.arrive(9)
    activate(2)
    tap(2)

    @pl.loop(0, 8)
    def _(i):
        base = pl.multiple_of(i * 128, 128)
        total = (
            taps[pl.ds(base, 128), 0:128]
            + taps[pl.ds(base + STEP, 128), 128:256]
            + taps[pl.ds(base + 2 * STEP, 128), 256:384]
        )
        cpre[pl.ds(base, 128), :] = total
        low = jax.nn.gelu(total).astype(BF16)
        mid[pl.ds(base, 128), :] = low
        midall[pl.ds(base, 128), pl.ds(pl.multiple_of(mine * 128, 128), 128)] = low

    ag_mid.begin()
    ag_pw.share()
    ag_pw.share_far()
    ag_mid.forward()
    swap_arrive(5)
    ag_cot.begin()
    ag_mid.share()
    ag_mid.share_far()
    ag_pw.arrive(6, 7, 8, 9)
    ag_cot.forward()
    ag_mid.arrive(6, 7, 8, 9)

    @pl.loop(0, 4)
    def _(i):
        rows = pl.ds(pl.multiple_of(i * 256, 256), 256)
        total = xall[rows, :].astype(F32) + dot_nn(midall[rows, :], pwall[...])
        low = total.astype(BF16)
        wide = low.astype(F32)
        normed[rows, :] = (wide * rms_scale(wide)).astype(BF16)

        @pl.when(i == p.y)
        def _():
            resid[...] = jnp.where(p.c == 0, low[0:128], low[128:256])

    pw_own[...] = pwall[pl.ds(pl.multiple_of(mine * 128, 128), 128), :]
    ag_cot.share()
    ag_cot.share_far()
    for k in (6, 7, 8):
        swap_arrive(k)

    @pl.loop(0, 4)
    def _(i):
        rows = pl.ds(pl.multiple_of(i * 256, 256), 256)
        tile = normed[rows, :]
        q_b[rows, :] = dot_nt(tile, wqkv[0:HSIZE, :]).astype(BF16)
        k_b[rows, :] = dot_nt(tile, wqkv[HSIZE : 2 * HSIZE, :]).astype(BF16)
        v_b[rows, :] = dot_nt(tile, wqkv[2 * HSIZE :, :]).astype(BF16)

    ag_cot.arrive(6, 7, 8, 9)
    swap_arrive(9)
    for k in range(len(swaps)):
        swap_copy(k).wait_send()
    for ag in (ag_x, ag_pw, ag_mid, ag_cot):
        ag.finish()
    dk_acc[...] = jnp.zeros_like(dk_acc)
    dv_acc[...] = jnp.zeros_like(dv_acc)

    @pl.loop(0, 4)
    def _(i):
        rows = pl.ds(pl.multiple_of(i * 256, 256), 256)
        tile = (cotall[rows, :].astype(F32) * inv_tokens).astype(BF16)
        cotall[rows, :] = tile
        gh_tile = dot_nt(tile, wo[...]).astype(BF16)
        q_tile = q_b[rows, :]
        ratio = jnp.tanh(dot_nt(q_tile, k_b[...]) * (INV_ROOT / SOFT_CAP))
        unnormed = jnp.exp(SOFT_CAP * ratio)
        weights = unnormed / jnp.sum(unnormed, axis=-1, keepdims=True)
        weights_low = weights.astype(BF16)
        att[rows, :] = dot_nn(weights_low, v_b[...]).astype(BF16)
        dv_acc[...] += dot_tn(weights_low, gh_tile)
        grad_soft = dot_nt(gh_tile, v_b[...])
        grad_capped = weights * (grad_soft - jnp.sum(weights * grad_soft, axis=-1, keepdims=True))
        score = (grad_capped * (1.0 - ratio * ratio)).astype(BF16)
        dcat[rows, 0:HSIZE] = (dot_nn(score, k_b[...]) * INV_ROOT).astype(BF16)
        dk_acc[...] += dot_tn(score, q_tile)

    dcat[:, HSIZE : 2 * HSIZE] = (dk_acc[...] * INV_ROOT).astype(BF16)
    dcat[:, 2 * HSIZE :] = dv_acc[...].astype(BF16)

    gn_part, op_part = pwall, xall
    rs_gn = Scatter(p, gn_part, near.at[0], made.at[0], land.at[0], rs_send.at[0], rs_recv.at[0])
    rs_op = Scatter(p, op_part, near.at[1], made.at[1], land.at[1], rs_send.at[1], rs_recv.at[1])
    for d in (2, 1, 3, 0):
        rows = pl.ds(pair_rows(d), 256)
        gn_part[rows, :] = dot_nn(dcat[rows, :], wqkv[...]).astype(BF16)
        rs_gn.copy(d).start()
    rs_gn.first()
    grad1, grad2 = red1[0], red2[0]

    @pl.loop(0, 4)
    def _(i):
        columns = pl.ds(pl.multiple_of(i * 384, 384), 384)
        value = dot_tn(normed[:, columns], dcat[...]).astype(BF16)
        grad1[pl.ds(2 * i, 2), :, :, :, 0:576] = value.reshape(2, 2, 2, 48, 576)
        value = dot_tn(cotall[:, columns], att[...]).astype(BF16)
        grad1[pl.ds(2 * i, 2), :, :, :, 576:768] = value.reshape(2, 2, 2, 48, HSIZE)

    rd1.begin()
    for d in (2, 1, 3, 0):
        rows = pl.ds(pair_rows(d), 256)
        op_part[rows, :] = dot_nn(att[rows, :], wo[...]).astype(BF16)
        rs_op.copy(d).start()
    rs_gn.second()
    rs_gn.total(rows_f32)

    own = pl.multiple_of(mine * ROWS, ROWS)

    @pl.loop(0, 4)
    def _(i):
        rows = pl.ds(pl.multiple_of(i * 32, 32), 32)
        total = rows_f32[rows, :]
        wide = resid[rows, :].astype(F32)
        scale = rms_scale(wide)
        gr[pl.ds(own + i * 32, 32), :] = (
            cotall[pl.ds(own + i * 32, 32), :].astype(F32)
            + scale * total
            - wide * scale**3 * jnp.mean(total * wide, axis=-1, keepdims=True)
        ).astype(BF16)

    ag_gr.begin()

    def conv_grad(d):
        base = pair_rows(d)
        rows = pl.ds(base, 256)
        value = gelu_back(cpre[rows, :], dot_nt(gr[rows, :], pw_own[...]))
        gpad[pl.ds(base + STEP, 256), :] = value.astype(BF16)

    ag_gr.arrive(6)
    conv_grad(0)
    ag_gr.forward()
    rd1.second()
    rs_op.first()
    ag_gr.share()
    ag_gr.arrive(7)
    conv_grad(3)
    ag_gr.arrive(8)
    conv_grad(1)
    rd1.third()
    ag_gr.share_far()
    ag_gr.arrive(9)
    conv_grad(2)
    moved[:, 0:INNER] = gpad[2 * STEP :, 0:INNER]
    moved[:, INNER : 2 * INNER] = gpad[STEP : LEN + STEP, 0:INNER]
    moved[:, 2 * INNER :] = gpad[0:LEN, 0:INNER]

    @pl.loop(0, 4)
    def _(i):
        columns = pl.ds(pl.multiple_of(i * 384, 384), 384)
        value = dot_tn(act[:, columns], moved[...]).astype(BF16)
        grad2[pl.ds(2 * i, 2), :, :, :, 0:288] = value.reshape(2, 2, 2, 48, 288)
        value = dot_tn(gr[:, columns], mid[...]).astype(BF16)
        grad2[pl.ds(2 * i, 2), :, :, :, 288:384] = value[:, 0:INNER].reshape(2, 2, 2, 48, INNER)

    rd2.begin()
    rs_op.second()
    rs_op.total(rows_f32)
    out_low[...] = (resid[...].astype(F32) + rows_f32[...]).astype(BF16)
    rd1.fourth()
    rd2.second()
    rd2.third()
    home = remote(out_low, out_home, home_send, home_recv, p.swap)
    home.start()
    rd2.fourth()
    rd1.finish()
    rd2.finish()
    home.wait_recv()
    home.wait_send()
    rs_gn.finish()
    rs_op.finish()
    ag_gr.finish()


def shape(*dims, dtype=BF16):
    return jax.ShapeDtypeStruct(dims, dtype)


def reduce_scratch(width):
    half = pltpu.VMEM((4, 2, 48, width), BF16)
    part = pltpu.VMEM((4, 48, width), BF16)
    return (
        pltpu.VMEM((8, 2, 2, 48, width), BF16), half, half, part, part, part, part,
        pltpu.VMEM((8, 48, width), BF16), pltpu.VMEM((7, 48, width), BF16), pltpu.VMEM((48, width), BF16),
    )


def layer(inv_tokens, x, dil, pw, cot, wq, wk, wv, wo):
    whole = pltpu.VMEM((LEN, CH), BF16)
    head = pltpu.VMEM((LEN, HSIZE), BF16)
    dma = pltpu.SemaphoreType.DMA
    return pl.pallas_call(
        functools.partial(layer_kernel, inv_tokens),
        name="layer",
        out_shape=(shape(ROWS, CH), shape(48, 768), shape(48, 384)),
        in_specs=[ANY_SPEC] * 8,
        out_specs=(VMEM_SPEC,) * 3,
        scratch_shapes=[
            whole, whole,
            pltpu.VMEM((LEN + 2 * STEP, 384), F32),
            pltpu.VMEM((LEN, 128), F32),
            pltpu.VMEM((LEN, 128), BF16),
            pltpu.VMEM((LEN, 1024), BF16),
            pltpu.VMEM((1024, CH), BF16),
            whole, whole,
            pltpu.VMEM((384, CH), BF16),
            pltpu.VMEM((3 * HSIZE, CH), BF16),
            pltpu.VMEM((HSIZE, CH), BF16),
            pltpu.VMEM((128, CH), BF16),
            pltpu.VMEM((ROWS, CH), BF16),
            head, head, head, pltpu.VMEM((8, 128), BF16), head,
            pltpu.VMEM((LEN, 3 * HSIZE), BF16),
            pltpu.VMEM((LEN, HSIZE), F32),
            pltpu.VMEM((LEN, HSIZE), F32),
            whole,
            pltpu.VMEM((LEN + 2 * STEP, 128), BF16),
            pltpu.VMEM((LEN, 3 * INNER), BF16),
            pltpu.VMEM((ROWS, CH), F32),
            pltpu.VMEM((ROWS, CH), BF16),
            pltpu.VMEM((2, 4, ROWS, CH), BF16),
            pltpu.VMEM((2, 6, 64, CH), BF16),
            pltpu.VMEM((2, 6, 64, CH), BF16),
            reduce_scratch(768),
            reduce_scratch(384),
            dma((10,)), dma((10,)), dma((5, 10)), dma((5, 10)), dma((2, 10)), dma((2, 10)),
            dma((2, 14)), dma((2, 14)), dma, dma,
        ],
        compiler_params=pltpu.CompilerParams(
            collective_id=0, has_side_effects=True, vmem_limit_bytes=LIMIT
        ),
    )(x, dil, pw, cot, wq, wk, wv, wo)


def shards(x, dil, pw, wq, wk, wv, wo, cot):
    inv_tokens = 1.0 / math.sqrt(BATCH * LEN)
    output, home1, home2 = layer(inv_tokens, x, dil, pw, cot, wq, wk, wv, wo)
    gq, gk, gv, go = jnp.split(home1.astype(F32), 4, axis=1)
    gd, gp = jnp.split(home2.astype(F32), [288], axis=1)
    return (
        output[None],
        gd.reshape(48, 3, INNER).transpose(1, 0, 2),
        gp.T,
        gq,
        gk,
        gv,
        go.T,
    )


def solution(mesh):
    torus = Mesh(mesh.devices.reshape(8, 2, 2, 4, 2), AXES)
    in_specs = (
        P(DP, SEQ, None),
        P(None, SEQ, None),
        P(SEQ, None),
        P(SEQ, None),
        P(SEQ, None),
        P(SEQ, None),
        P(SEQ, None),
        P(DP, SEQ, None),
    )
    out_specs = (
        P(DP, SEQ, None),
        P(None, DP, SEQ),
        P(SEQ, DP),
        P(DP, SEQ),
        P(DP, SEQ),
        P(DP, SEQ),
        P(SEQ, DP),
    )
    return jax.shard_map(
        shards, mesh=torus, in_specs=in_specs, out_specs=out_specs, check_vma=False
    )
```

```python
import functools
import math

import jax
import jax.numpy as jnp
from jax import lax
from jax.experimental import pallas as pl
from jax.experimental.pallas import tpu as pltpu
from jax.sharding import Mesh
from jax.sharding import PartitionSpec as P

HSIZE = 192
STEP = 16
EPSILON = 1e-06
SOFT_CAP = 6.0
LEN = 1024
CH = 1536
INNER = 96
ROWS = 128
BATCH = 32
AXES = ("z", "xl", "c", "y", "xh")
DP = ("z", "xl", "c")
SEQ = ("y", "xh")
MESH_ID = pl.DeviceIdType.MESH
F32 = jnp.float32
BF16 = jnp.bfloat16
VMEM_SPEC = pl.BlockSpec(memory_space=pltpu.VMEM)
ANY_SPEC = pl.BlockSpec(memory_space=pl.ANY)
LIMIT = 62 * 1024 * 1024


def dot_nt(a, b):
    return lax.dot_general(a, b, (((1,), (1,)), ((), ())), preferred_element_type=F32)


def dot_nn(a, b):
    return jnp.dot(a, b, preferred_element_type=F32)


def dot_tn(a, b):
    return lax.dot_general(a, b, (((0,), (0,)), ((), ())), preferred_element_type=F32)


def rms_scale(rows):
    return lax.rsqrt(jnp.mean(rows * rows, axis=-1, keepdims=True) + EPSILON)


def gelu_back(pre_act, upstream):
    return jax.vjp(jax.nn.gelu, pre_act)[1](upstream)[0]


class Place:
    def __init__(self):
        self.z = lax.axis_index("z")
        self.xl = lax.axis_index("xl")
        self.c = lax.axis_index("c")
        self.y = lax.axis_index("y")
        self.xh = lax.axis_index("xh")
        self.up = {"y": lax.rem(self.y + 1, 4)}
        self.down = {"y": lax.rem(self.y + 3, 4)}
        self.twin = {"c": 1 - self.c}
        self.swap = {"xl": 1 - self.xl, "xh": self.c, "c": self.xh}

    def block(self, d, mine=True):
        return lax.rem(self.y + d, 4) * 2 + (self.c if mine else 1 - self.c)


def greet(devices):
    barrier = pltpu.get_barrier_semaphore()
    for device in devices:
        pl.semaphore_signal(barrier, inc=1, device_id=device, device_id_type=MESH_ID)
    pl.semaphore_wait(barrier, len(devices))


def remote(src, dst, send, recv, device):
    return pltpu.make_async_remote_copy(
        src_ref=src, dst_ref=dst, send_sem=send, recv_sem=recv,
        device_id=device, device_id_type=MESH_ID,
    )


class Gather:
    def __init__(self, place, view, send, recv):
        self.view, self.send, self.recv = view, send, recv
        p = place
        own, low, high, far = (p.block(d) for d in (0, 3, 1, 2))
        own2, low2, high2, far2 = (p.block(d, False) for d in (0, 3, 1, 2))
        self.out = [
            (own, 0, p.up), (own, 1, p.up), (low, 0, p.up),
            (own, 1, p.down), (own, 0, p.down), (high, 1, p.down),
            (own, None, p.twin), (low, None, p.twin), (high, None, p.twin), (far, None, p.twin),
        ]
        self.inn = [
            (low, 0), (low, 1), (far, 0), (high, 1), (high, 0), (far, 1),
            (own2, None), (low2, None), (high2, None), (far2, None),
        ]

    def copy(self, k):
        block, half, device = self.out[k]
        ref = self.view(block, half)
        return remote(ref, ref, self.send.at[k], self.recv.at[k], device)

    def start(self, *ks):
        for k in ks:
            self.copy(k).start()

    def arrive(self, *ks):
        for k in ks:
            block, half = self.inn[k]
            ref = self.view(block, half)
            remote(ref, ref, self.send.at[k], self.recv.at[k], self.out[k][2]).wait_recv()

    def begin(self):
        self.start(0, 3, 1, 4, 6)

    def forward(self):
        self.arrive(0)
        self.start(2)
        self.arrive(3)
        self.start(5)

    def share(self):
        self.arrive(1)
        self.start(7)
        self.arrive(4)
        self.start(8)

    def share_far(self):
        self.arrive(2, 5)
        self.start(9)

    def finish(self):
        for k in range(10):
            self.copy(k).wait_send()


def row_view(ref, pitch, rows):
    def view(block, half):
        if half is None:
            return ref.at[pl.ds(pl.multiple_of(block * pitch, pitch), rows)]
        start = pl.multiple_of(block * pitch + half * (rows // 2), 16)
        return ref.at[pl.ds(start, rows // 2)]
    return view


def column_view(ref):
    def view(block, half):
        columns = pl.ds(pl.multiple_of(block * 128, 128), 128)
        if half is None:
            return ref.at[:, columns]
        return ref.at[pl.ds(half * (LEN // 2), LEN // 2), columns]
    return view


def spot(p, d, side):
    core = p.c if side == 0 else 1 - p.c
    y = lax.rem(p.y + d, 4)
    return y * 2 + core, ({"y": y} if side == 0 else {"y": y, "c": core})


class Scatter:
    def __init__(self, place, part, near, made, land, send, recv):
        self.p, self.part, self.near, self.made, self.land = place, part, near, made, land
        self.send, self.recv = send, recv

    def own_rows(self, d, half):
        start = pl.multiple_of(self.p.block(d) * ROWS + half * 64, 64)
        return self.part[pl.ds(start, 64), :].astype(F32)

    def both(self, d, half):
        rows = slice(half * 64, half * 64 + 64)
        return self.own_rows(d, half) + self.near[d, rows, :].astype(F32)

    def copies(self, k):
        p = self.p
        if k < 4:
            start = pl.multiple_of(p.block(k, False) * ROWS, ROWS)
            return self.part.at[pl.ds(start, ROWS)], self.near.at[k], p.twin
        d, half, device = [
            (2, 0, p.down), (2, 1, p.up), (1, 0, p.up), (3, 1, p.down), (3, 0, p.down), (1, 1, p.up)
        ][k - 4]
        return self.made.at[k - 4], self.land.at[k - 4], device

    def copy(self, k):
        src, dst, device = self.copies(k)
        return remote(src, dst, self.send.at[k], self.recv.at[k], device)

    def begin(self):
        for d in (2, 1, 3, 0):
            self.copy(d).start()

    def make(self, k, value):
        self.made[k - 4, :, :] = value.astype(BF16)
        self.copy(k).start()

    def first(self):
        self.copy(2).wait_recv()
        self.make(4, self.both(2, 0))
        self.make(5, self.both(2, 1))
        self.copy(1).wait_recv()
        self.make(6, self.both(1, 0))
        self.copy(3).wait_recv()
        self.make(7, self.both(3, 1))

    def second(self):
        self.copy(4).wait_recv()
        self.make(8, self.both(3, 0) + self.land[0].astype(F32))
        self.copy(5).wait_recv()
        self.make(9, self.both(1, 1) + self.land[1].astype(F32))

    def total(self, out):
        self.copy(0).wait_recv()
        for k in (6, 7, 8, 9):
            self.copy(k).wait_recv()
        out[0:64, :] = self.both(0, 0) + self.land[2].astype(F32) + self.land[4].astype(F32)
        out[64:128, :] = self.both(0, 1) + self.land[3].astype(F32) + self.land[5].astype(F32)

    def finish(self):
        for k in range(10):
            self.copy(k).wait_send()


class Reduce:
    def __init__(self, place, grad, r1a, r1b, sa, sb, r2a, r2b, quarter, landed, final, home, send, recv):
        self.p, self.grad = place, grad
        self.r1a, self.r1b, self.sa, self.sb, self.r2a, self.r2b = r1a, r1b, sa, sb, r2a, r2b
        self.quarter, self.landed, self.final, self.home = quarter, landed, final, home
        self.send, self.recv = send, recv
        p = place
        self.near = {"xl": 1 - p.xl}
        self.cross = {"xl": 1 - p.xl, "xh": 1 - p.xh}
        odd = lax.rem(p.xl + p.xh, 2)
        self.keep = [lax.rem(odd + 1 - k, 2) for k in range(2)]

    def copy(self, k):
        p = self.p
        if k < 2:
            src, dst, device = self.grad.at[pl.ds(0, 4), k, 1 - self.keep[k]], self.r1a.at[:, k], self.near
        elif k < 4:
            src, dst, device = self.grad.at[pl.ds(4, 4), k - 2, 1 - p.xh], self.r1b.at[:, k - 2], self.cross
        elif k == 4:
            src, dst, device = self.sa, self.r2a, self.cross
        elif k == 5:
            src, dst, device = self.sb, self.r2b, self.near
        elif k < 13:
            dz = k - 5
            target = lax.rem(p.z + dz, 8)
            src, dst, device = self.quarter.at[target], self.landed.at[dz - 1], {"z": target}
        else:
            src, dst, device = self.final, self.home, p.swap
        return remote(src, dst, self.send.at[k], self.recv.at[k], device)

    def begin(self):
        for k in range(4):
            self.copy(k).start()

    def second(self):
        p = self.p
        for k in range(4):
            self.copy(k).wait_recv()
        keep = [self.grad[0:4, k, self.keep[k]].astype(F32) + self.r1a[:, k].astype(F32) for k in range(2)]
        mine = p.xl == 0
        self.sa[...] = jnp.where(mine, keep[0], keep[1]).astype(BF16)
        self.copy(4).start()
        self.quarter[0:4] = jnp.where(mine, keep[1], keep[0]).astype(BF16)
        keep = [self.grad[4:8, k, p.xh].astype(F32) + self.r1b[:, k].astype(F32) for k in range(2)]
        self.sb[...] = jnp.where(mine, keep[0], keep[1]).astype(BF16)
        self.copy(5).start()
        self.quarter[4:8] = jnp.where(mine, keep[1], keep[0]).astype(BF16)

    def third(self):
        self.copy(4).wait_recv()
        self.quarter[0:4] = (self.quarter[0:4].astype(F32) + self.r2a[...].astype(F32)).astype(BF16)
        self.copy(5).wait_recv()
        self.quarter[4:8] = (self.quarter[4:8].astype(F32) + self.r2b[...].astype(F32)).astype(BF16)
        for dz in (4, 3, 5, 2, 6, 1, 7):
            self.copy(5 + dz).start()

    def fourth(self):
        total = self.quarter[self.p.z].astype(F32)
        for dz in range(1, 8):
            self.copy(5 + dz).wait_recv()
            total = total + self.landed[dz - 1].astype(F32)
        self.final[...] = total.astype(BF16)
        self.copy(13).start()

    def finish(self):
        self.copy(13).wait_recv()
        for k in range(14):
            self.copy(k).wait_send()


INV_ROOT = 1.0 / math.sqrt(HSIZE)


def layer_kernel(
    inv_tokens,
    x_ref, dil_ref, pw_ref, cot_ref, wq_ref, wk_ref, wv_ref, wo_ref,
    out_home, home1, home2, home3,
    xall, act, taps, cpre, mid, midall, pwall, cotall, normed, dil, wqkv, wo, resid, op_part,
    q_b, k_b, v_b, att, dcat, dk_acc, dv_acc, gr, gms, gmr, gpad, moved, rows_f32, out_low,
    near, made, land, red1, red2, red3,
    swap_send, swap_recv, ag_send, ag_recv, rs_send, rs_recv, rd_send, rd_recv, gm_send, gm_recv, home_send, home_recv,
):
    p = Place()
    mine = p.block(0)
    there = p.y * 2 + p.xh
    taps[0:STEP, :] = jnp.zeros((STEP, 384), F32)
    taps[LEN + STEP :, :] = jnp.zeros((STEP, 384), F32)
    gpad[0:STEP, :] = jnp.zeros((STEP, 128), BF16)
    gpad[LEN + STEP :, :] = jnp.zeros((STEP, 128), BF16)
    for j in range(8):
        pwall[j * 128 + INNER : (j + 1) * 128, :] = jnp.zeros((32, CH), BF16)
    for k in range(3):
        dil[k * 128 + INNER : (k + 1) * 128, :] = jnp.zeros((32, CH), BF16)

    rd1 = Reduce(p, *red1, home1, rd_send.at[0], rd_recv.at[0])
    rd2 = Reduce(p, *red2, home2, rd_send.at[1], rd_recv.at[1])
    rd3 = Reduce(p, *red3, home3, rd_send.at[2], rd_recv.at[2])
    greet(
        [p.swap, rd1.near, rd1.cross, p.twin]
        + [spot(p, d, side)[1] for d in (1, 2, 3) for side in (0, 1)]
        + [{"z": lax.rem(p.z + dz, 8)} for dz in range(1, 8)]
    )

    def at(ref, block, pitch, rows):
        return ref.at[pl.ds(pl.multiple_of(block * pitch, pitch), rows)]

    def piece(ref, k, rows):
        return ref.at[pl.ds(k, rows)]

    swaps = [
        (x_ref.at[0], at(xall, there, ROWS, ROWS), at(xall, mine, ROWS, ROWS)),
        *[(dil_ref.at[k], piece(dil, k * 128, INNER), piece(dil, k * 128, INNER)) for k in range(3)],
        (pw_ref, at(pwall, there, 128, INNER), at(pwall, mine, 128, INNER)),
        (cot_ref.at[0], at(cotall, there, ROWS, ROWS), at(cotall, mine, ROWS, ROWS)),
        (wq_ref, piece(wqkv, 0, HSIZE), piece(wqkv, 0, HSIZE)),
        (wk_ref, piece(wqkv, HSIZE, HSIZE), piece(wqkv, HSIZE, HSIZE)),
        (wv_ref, piece(wqkv, 2 * HSIZE, HSIZE), piece(wqkv, 2 * HSIZE, HSIZE)),
        (wo_ref, wo, wo),
    ]

    def swap_copy(k):
        src, dst, _ = swaps[k]
        return remote(src, dst, swap_send.at[k], swap_recv.at[k], p.swap)

    def swap_arrive(k):
        src, _, here = swaps[k]
        remote(src, here, swap_send.at[k], swap_recv.at[k], p.swap).wait_recv()

    for k in range(len(swaps)):
        swap_copy(k).start()

    ag_x = Gather(p, row_view(xall, ROWS, ROWS), ag_send.at[0], ag_recv.at[0])
    ag_pw = Gather(p, row_view(pwall, 128, INNER), ag_send.at[1], ag_recv.at[1])
    ag_mid = Gather(p, column_view(midall), ag_send.at[2], ag_recv.at[2])
    ag_cot = Gather(p, row_view(cotall, ROWS, ROWS), ag_send.at[3], ag_recv.at[3])
    ag_gr = Gather(p, row_view(gr, ROWS, ROWS), ag_send.at[4], ag_recv.at[4])

    def pair_rows(d):
        return pl.multiple_of(lax.rem(p.y + d, 4) * 256, 256)

    def activate(d):
        base = pair_rows(d)

        @pl.loop(0, 8)
        def _(i):
            rows = pl.ds(pl.multiple_of(base + i * 32, 32), 32)
            value = xall[rows, :].astype(F32)
            act[rows, :] = jax.nn.gelu(value * rms_scale(value)).astype(BF16)

    def tap(d):
        base = pair_rows(d)
        taps[pl.ds(base + STEP, 256), :] = dot_nt(act[pl.ds(base, 256), :], dil[...])

    swap_arrive(0)
    ag_x.begin()
    ag_x.arrive(6)
    activate(0)
    ag_x.forward()
    ag_x.share()
    for k in (1, 2, 3):
        swap_arrive(k)
    tap(0)
    ag_x.arrive(7)
    activate(3)
    tap(3)
    ag_x.share_far()
    swap_arrive(4)
    ag_pw.begin()
    ag_x.arrive(8)
    activate(1)
    tap(1)
    ag_pw.forward()
    ag_x.arrive(9)
    activate(2)
    tap(2)

    @pl.loop(0, 8)
    def _(i):
        base = pl.multiple_of(i * 128, 128)
        total = (
            taps[pl.ds(base, 128), 0:128]
            + taps[pl.ds(base + STEP, 128), 128:256]
            + taps[pl.ds(base + 2 * STEP, 128), 256:384]
        )
        cpre[pl.ds(base, 128), :] = total
        low = jax.nn.gelu(total).astype(BF16)
        mid[pl.ds(base, 128), :] = low
        midall[pl.ds(base, 128), pl.ds(pl.multiple_of(mine * 128, 128), 128)] = low

    ag_mid.begin()
    ag_pw.share()
    ag_pw.share_far()
    ag_mid.forward()
    swap_arrive(5)
    ag_cot.begin()
    ag_mid.share()
    ag_mid.share_far()
    ag_pw.arrive(6, 7, 8, 9)
    ag_mid.arrive(6, 7, 8, 9)

    @pl.loop(0, 4)
    def _(i):
        rows = pl.ds(pl.multiple_of(i * 256, 256), 256)
        total = xall[rows, :].astype(F32) + dot_nn(midall[rows, :], pwall[...])
        low = total.astype(BF16)
        wide = low.astype(F32)
        normed[rows, :] = (wide * rms_scale(wide)).astype(BF16)

        @pl.when(i == p.y)
        def _():
            resid[...] = jnp.where(p.c == 0, low[0:128], low[128:256])

    ag_cot.forward()
    for k in (6, 7, 8):
        swap_arrive(k)

    @pl.loop(0, 4)
    def _(i):
        rows = pl.ds(pl.multiple_of(i * 256, 256), 256)
        tile = normed[rows, :]
        q_b[rows, :] = dot_nt(tile, wqkv[0:HSIZE, :]).astype(BF16)
        k_b[rows, :] = dot_nt(tile, wqkv[HSIZE : 2 * HSIZE, :]).astype(BF16)
        v_b[rows, :] = dot_nt(tile, wqkv[2 * HSIZE :, :]).astype(BF16)

    ag_cot.share()
    swap_arrive(9)
    dk_acc[...] = jnp.zeros_like(dk_acc)
    dv_acc[...] = jnp.zeros_like(dv_acc)

    def attend(d):
        rows = pl.ds(pair_rows(d), 256)
        gh_tile = (dot_nt(cotall[rows, :], wo[...]) * inv_tokens).astype(BF16)
        q_tile = q_b[rows, :]
        ratio = jnp.tanh(dot_nt(q_tile, k_b[...]) * (INV_ROOT / SOFT_CAP))
        unnormed = jnp.exp(SOFT_CAP * ratio)
        weights = unnormed / jnp.sum(unnormed, axis=-1, keepdims=True)
        weights_low = weights.astype(BF16)
        att[rows, :] = dot_nn(weights_low, v_b[...]).astype(BF16)
        dv_acc[...] += dot_tn(weights_low, gh_tile)
        grad_soft = dot_nt(gh_tile, v_b[...])
        grad_capped = weights * (grad_soft - jnp.sum(weights * grad_soft, axis=-1, keepdims=True))
        score = (grad_capped * (1.0 - ratio * ratio)).astype(BF16)
        dcat[rows, 0:HSIZE] = (dot_nn(score, k_b[...]) * INV_ROOT).astype(BF16)
        dk_acc[...] += dot_tn(score, q_tile)

    ag_cot.arrive(6)
    attend(0)
    ag_cot.arrive(7)
    attend(3)
    ag_cot.share_far()
    ag_cot.arrive(8)
    attend(1)
    ag_cot.arrive(9)
    attend(2)
    ag_x.finish()
    dcat[:, HSIZE : 2 * HSIZE] = (dk_acc[...] * INV_ROOT).astype(BF16)
    dcat[:, 2 * HSIZE :] = dv_acc[...].astype(BF16)

    gn_part = xall
    rs_gn = Scatter(p, gn_part, near.at[0], made.at[0], land.at[0], rs_send.at[0], rs_recv.at[0])
    rs_op = Scatter(p, op_part, near.at[1], made.at[1], land.at[1], rs_send.at[1], rs_recv.at[1])
    for d in (2, 1, 3, 0):
        rows = pl.ds(pair_rows(d), 256)
        gn_part[rows, :] = dot_nn(dcat[rows, :], wqkv[...]).astype(BF16)
        rs_gn.copy(d).start()
    rs_gn.first()
    grad1, grad2, grad3 = red1[0], red2[0], red3[0]

    @pl.loop(0, 4)
    def _(i):
        columns = pl.ds(pl.multiple_of(i * 384, 384), 384)
        value = dot_tn(normed[:, columns], dcat[...]).astype(BF16)
        grad1[pl.ds(2 * i, 2), :, :, :, 0:576] = value.reshape(2, 2, 2, 48, 576)
        value = (dot_tn(cotall[:, columns], att[...]) * inv_tokens).astype(BF16)
        grad1[pl.ds(2 * i, 2), :, :, :, 576:768] = value.reshape(2, 2, 2, 48, HSIZE)

    rd1.begin()
    for d in (2, 1, 3, 0):
        rows = pl.ds(pair_rows(d), 256)
        op_part[rows, :] = dot_nn(att[rows, :], wo[...]).astype(BF16)
        rs_op.copy(d).start()
    rs_gn.second()
    rs_gn.total(rows_f32)

    own = pl.multiple_of(mine * ROWS, ROWS)

    @pl.loop(0, 4)
    def _(i):
        rows = pl.ds(pl.multiple_of(i * 32, 32), 32)
        total = rows_f32[rows, :]
        wide = resid[rows, :].astype(F32)
        scale = rms_scale(wide)
        gr[pl.ds(own + i * 32, 32), :] = (
            cotall[pl.ds(own + i * 32, 32), :].astype(F32) * inv_tokens
            + scale * total
            - wide * scale**3 * jnp.mean(total * wide, axis=-1, keepdims=True)
        ).astype(BF16)

    gm_value = dot_nt(gr[pl.ds(own, ROWS), :], pwall[...]).astype(BF16)
    for j in range(8):
        gms[j, :, :] = gm_value[:, j * 128 : (j + 1) * 128]
    spots = [(d, side) for d in (2, 1, 3, 0) for side in (0, 1) if (d, side) != (0, 0)]

    def gm_copy(k):
        block, device = spot(p, *spots[k])
        return remote(gms.at[block], gmr.at[pl.ds(own, ROWS)], gm_send.at[k], gm_recv.at[k], device)

    def gm_arrive(k):
        d, side = spots[k]
        block, device = spot(p, (4 - d) % 4, side)
        here = gmr.at[pl.ds(pl.multiple_of(block * ROWS, ROWS), ROWS)]
        remote(gms.at[0], here, gm_send.at[k], gm_recv.at[k], device).wait_recv()

    for k in range(7):
        gm_copy(k).start()
    ag_gr.begin()
    gmr[pl.ds(own, ROWS), :] = gms[mine]
    rd1.second()
    for k in range(7):
        gm_arrive(k)

    @pl.loop(0, 8)
    def _(i):
        rows = pl.ds(pl.multiple_of(i * 128, 128), 128)
        value = gelu_back(cpre[rows, :], gmr[rows, :].astype(F32))
        gpad[pl.ds(pl.multiple_of(i * 128 + STEP, STEP), 128), :] = value.astype(BF16)

    moved[:, 0:INNER] = gpad[2 * STEP :, 0:INNER]
    moved[:, INNER : 2 * INNER] = gpad[STEP : LEN + STEP, 0:INNER]
    moved[:, 2 * INNER :] = gpad[0:LEN, 0:INNER]

    @pl.loop(0, 4)
    def _(i):
        columns = pl.ds(pl.multiple_of(i * 384, 384), 384)
        value = dot_tn(act[:, columns], moved[...]).astype(BF16)
        grad2[pl.ds(2 * i, 2)] = value.reshape(2, 2, 2, 48, 3 * INNER)

    rd2.begin()
    ag_gr.forward()
    rs_op.first()
    ag_gr.share()
    rd1.third()
    ag_gr.share_far()
    rd2.second()
    ag_gr.arrive(6, 7, 8, 9)

    @pl.loop(0, 4)
    def _(i):
        columns = pl.ds(pl.multiple_of(i * 384, 384), 384)
        value = dot_tn(gr[:, columns], mid[...]).astype(BF16)
        grad3[pl.ds(2 * i, 2)] = value.reshape(2, 2, 2, 48, 128)

    rd3.begin()
    rd2.third()
    rs_op.second()
    rs_op.total(rows_f32)
    out_low[...] = (resid[...].astype(F32) + rows_f32[...]).astype(BF16)
    rd3.second()
    home = remote(out_low, out_home, home_send, home_recv, p.swap)
    home.start()
    rd3.third()
    rd1.fourth()
    rd2.fourth()
    rd3.fourth()
    for rd in (rd1, rd2, rd3):
        rd.finish()
    home.wait_recv()
    home.wait_send()
    for k in range(len(swaps)):
        swap_copy(k).wait_send()
    for k in range(7):
        gm_copy(k).wait_send()
    for part in (rs_gn, rs_op, ag_pw, ag_mid, ag_cot, ag_gr):
        part.finish()


def shape(*dims, dtype=BF16):
    return jax.ShapeDtypeStruct(dims, dtype)


def reduce_scratch(width):
    half = pltpu.VMEM((4, 2, 48, width), BF16)
    part = pltpu.VMEM((4, 48, width), BF16)
    return (
        pltpu.VMEM((8, 2, 2, 48, width), BF16), half, half, part, part, part, part,
        pltpu.VMEM((8, 48, width), BF16), pltpu.VMEM((7, 48, width), BF16), pltpu.VMEM((48, width), BF16),
    )


def layer(inv_tokens, x, dil, pw, cot, wq, wk, wv, wo):
    whole = pltpu.VMEM((LEN, CH), BF16)
    head = pltpu.VMEM((LEN, HSIZE), BF16)
    dma = pltpu.SemaphoreType.DMA
    return pl.pallas_call(
        functools.partial(layer_kernel, inv_tokens),
        name="layer",
        out_shape=(shape(ROWS, CH), shape(48, 768), shape(48, 288), shape(48, 128)),
        in_specs=[ANY_SPEC] * 8,
        out_specs=(VMEM_SPEC,) * 4,
        scratch_shapes=[
            whole, whole,
            pltpu.VMEM((LEN + 2 * STEP, 384), F32),
            pltpu.VMEM((LEN, 128), F32),
            pltpu.VMEM((LEN, 128), BF16),
            pltpu.VMEM((LEN, 1024), BF16),
            pltpu.VMEM((1024, CH), BF16),
            whole, whole,
            pltpu.VMEM((384, CH), BF16),
            pltpu.VMEM((3 * HSIZE, CH), BF16),
            pltpu.VMEM((HSIZE, CH), BF16),
            pltpu.VMEM((ROWS, CH), BF16),
            whole,
            head, head, head, head,
            pltpu.VMEM((LEN, 3 * HSIZE), BF16),
            pltpu.VMEM((LEN, HSIZE), F32),
            pltpu.VMEM((LEN, HSIZE), F32),
            whole,
            pltpu.VMEM((8, 128, 128), BF16),
            pltpu.VMEM((LEN, 128), BF16),
            pltpu.VMEM((LEN + 2 * STEP, 128), BF16),
            pltpu.VMEM((LEN, 3 * INNER), BF16),
            pltpu.VMEM((ROWS, CH), F32),
            pltpu.VMEM((ROWS, CH), BF16),
            pltpu.VMEM((2, 4, ROWS, CH), BF16),
            pltpu.VMEM((2, 6, 64, CH), BF16),
            pltpu.VMEM((2, 6, 64, CH), BF16),
            reduce_scratch(768),
            reduce_scratch(288),
            reduce_scratch(128),
            dma((10,)), dma((10,)), dma((5, 10)), dma((5, 10)), dma((2, 10)), dma((2, 10)),
            dma((3, 14)), dma((3, 14)), dma((7,)), dma((7,)), dma, dma,
        ],
        compiler_params=pltpu.CompilerParams(
            collective_id=0, has_side_effects=True, vmem_limit_bytes=LIMIT
        ),
    )(x, dil, pw, cot, wq, wk, wv, wo)


def split_kernel(low, h1, h2, h3, output, gd, gp, gq, gk, gv, go):
    output[0] = low[...]
    wide = h1[...].astype(F32)
    gq[...] = wide[:, 0:HSIZE]
    gk[...] = wide[:, HSIZE : 2 * HSIZE]
    gv[...] = wide[:, 2 * HSIZE : 3 * HSIZE]
    go[...] = wide[:, 3 * HSIZE :].T
    taps = h2[...].astype(F32)
    for k in range(3):
        gd[k] = taps[:, k * INNER : (k + 1) * INNER]
    gp[...] = h3[...].astype(F32)[:, 0:INNER].T


def shards(x, dil, pw, wq, wk, wv, wo, cot):
    inv_tokens = 1.0 / math.sqrt(BATCH * LEN)
    homes = layer(inv_tokens, x, dil, pw, cot, wq, wk, wv, wo)
    square = shape(48, HSIZE, dtype=F32)
    return pl.pallas_call(
        split_kernel,
        name="split",
        out_shape=(
            shape(1, ROWS, CH), shape(3, 48, INNER, dtype=F32), shape(INNER, 48, dtype=F32),
            square, square, square, shape(HSIZE, 48, dtype=F32),
        ),
        in_specs=[VMEM_SPEC] * 4,
        out_specs=(VMEM_SPEC,) * 7,
    )(*homes)


def solution(mesh):
    torus = Mesh(mesh.devices.reshape(8, 2, 2, 4, 2), AXES)
    in_specs = (
        P(DP, SEQ, None),
        P(None, SEQ, None),
        P(SEQ, None),
        P(SEQ, None),
        P(SEQ, None),
        P(SEQ, None),
        P(SEQ, None),
        P(DP, SEQ, None),
    )
    out_specs = (
        P(DP, SEQ, None),
        P(None, DP, SEQ),
        P(SEQ, DP),
        P(DP, SEQ),
        P(DP, SEQ),
        P(DP, SEQ),
        P(SEQ, DP),
    )
    return jax.shard_map(
        shards, mesh=torus, in_specs=in_specs, out_specs=out_specs, check_vma=False
    )
```

```python
import functools
import math

import jax
import jax.numpy as jnp
from jax import lax
from jax.experimental import pallas as pl
from jax.experimental.pallas import tpu as pltpu
from jax.sharding import Mesh
from jax.sharding import PartitionSpec as P

HSIZE = 192
STEP = 16
EPSILON = 1e-06
SOFT_CAP = 6.0
LEN = 1024
CH = 1536
INNER = 96
ROWS = 128
BATCH = 32
AXES = ("z", "xl", "c", "y", "xh")
DP = ("z", "xl", "c")
SEQ = ("y", "xh")
MESH_ID = pl.DeviceIdType.MESH
F32 = jnp.float32
BF16 = jnp.bfloat16
VMEM_SPEC = pl.BlockSpec(memory_space=pltpu.VMEM)
ANY_SPEC = pl.BlockSpec(memory_space=pl.ANY)
LIMIT = 62 * 1024 * 1024


def dot_nt(a, b):
    return lax.dot_general(a, b, (((1,), (1,)), ((), ())), preferred_element_type=F32)


def dot_nn(a, b):
    return jnp.dot(a, b, preferred_element_type=F32)


def dot_tn(a, b):
    return lax.dot_general(a, b, (((0,), (0,)), ((), ())), preferred_element_type=F32)


def rms_scale(rows):
    return lax.rsqrt(jnp.mean(rows * rows, axis=-1, keepdims=True) + EPSILON)


def gelu_back(pre_act, upstream):
    return jax.vjp(jax.nn.gelu, pre_act)[1](upstream)[0]


class Place:
    def __init__(self):
        self.z = lax.axis_index("z")
        self.xl = lax.axis_index("xl")
        self.c = lax.axis_index("c")
        self.y = lax.axis_index("y")
        self.xh = lax.axis_index("xh")
        self.up = {"y": lax.rem(self.y + 1, 4)}
        self.down = {"y": lax.rem(self.y + 3, 4)}
        self.twin = {"c": 1 - self.c}
        self.swap = {"xl": 1 - self.xl, "xh": self.c, "c": self.xh}

    def block(self, d, mine=True):
        return lax.rem(self.y + d, 4) * 2 + (self.c if mine else 1 - self.c)


def greet(devices):
    barrier = pltpu.get_barrier_semaphore()
    for device in devices:
        pl.semaphore_signal(barrier, inc=1, device_id=device, device_id_type=MESH_ID)
    pl.semaphore_wait(barrier, len(devices))


def remote(src, dst, send, recv, device):
    return pltpu.make_async_remote_copy(
        src_ref=src, dst_ref=dst, send_sem=send, recv_sem=recv,
        device_id=device, device_id_type=MESH_ID,
    )


class Gather:
    def __init__(self, place, view, send, recv):
        self.view, self.send, self.recv = view, send, recv
        p = place
        own, low, high, far = (p.block(d) for d in (0, 3, 1, 2))
        own2, low2, high2, far2 = (p.block(d, False) for d in (0, 3, 1, 2))
        self.out = [
            (own, 0, p.up), (own, 1, p.up), (low, 0, p.up),
            (own, 1, p.down), (own, 0, p.down), (high, 1, p.down),
            (own, None, p.twin), (low, None, p.twin), (high, None, p.twin), (far, None, p.twin),
        ]
        self.inn = [
            (low, 0), (low, 1), (far, 0), (high, 1), (high, 0), (far, 1),
            (own2, None), (low2, None), (high2, None), (far2, None),
        ]

    def copy(self, k):
        block, half, device = self.out[k]
        ref = self.view(block, half)
        return remote(ref, ref, self.send.at[k], self.recv.at[k], device)

    def start(self, *ks):
        for k in ks:
            self.copy(k).start()

    def arrive(self, *ks):
        for k in ks:
            block, half = self.inn[k]
            ref = self.view(block, half)
            remote(ref, ref, self.send.at[k], self.recv.at[k], self.out[k][2]).wait_recv()

    def begin(self):
        self.start(0, 3, 1, 4, 6)

    def forward(self):
        self.arrive(0)
        self.start(2)
        self.arrive(3)
        self.start(5)

    def share(self):
        self.arrive(1)
        self.start(7)
        self.arrive(4)
        self.start(8)

    def share_far(self):
        self.arrive(2, 5)
        self.start(9)

    def finish(self):
        for k in range(10):
            self.copy(k).wait_send()


def row_view(ref, pitch, rows):
    def view(block, half):
        if half is None:
            return ref.at[pl.ds(pl.multiple_of(block * pitch, pitch), rows)]
        start = pl.multiple_of(block * pitch + half * (rows // 2), 16)
        return ref.at[pl.ds(start, rows // 2)]
    return view


def column_view(ref):
    def view(block, half):
        columns = pl.ds(pl.multiple_of(block * 128, 128), 128)
        if half is None:
            return ref.at[:, columns]
        return ref.at[pl.ds(half * (LEN // 2), LEN // 2), columns]
    return view


def spot(p, d, side):
    core = p.c if side == 0 else 1 - p.c
    y = lax.rem(p.y + d, 4)
    return y * 2 + core, ({"y": y} if side == 0 else {"y": y, "c": core})


class Scatter:
    def __init__(self, place, part, near, made, land, send, recv):
        self.p, self.part, self.near, self.made, self.land = place, part, near, made, land
        self.send, self.recv = send, recv

    def own_rows(self, d, half):
        start = pl.multiple_of(self.p.block(d) * ROWS + half * 64, 64)
        return self.part[pl.ds(start, 64), :].astype(F32)

    def both(self, d, half):
        rows = slice(half * 64, half * 64 + 64)
        return self.own_rows(d, half) + self.near[d, rows, :].astype(F32)

    def copies(self, k):
        p = self.p
        if k < 4:
            start = pl.multiple_of(p.block(k, False) * ROWS, ROWS)
            return self.part.at[pl.ds(start, ROWS)], self.near.at[k], p.twin
        d, half, device = [
            (2, 0, p.down), (2, 1, p.up), (1, 0, p.up), (3, 1, p.down), (3, 0, p.down), (1, 1, p.up)
        ][k - 4]
        return self.made.at[k - 4], self.land.at[k - 4], device

    def copy(self, k):
        src, dst, device = self.copies(k)
        return remote(src, dst, self.send.at[k], self.recv.at[k], device)

    def begin(self):
        for d in (2, 1, 3, 0):
            self.copy(d).start()

    def make(self, k, value):
        self.made[k - 4, :, :] = value.astype(BF16)
        self.copy(k).start()

    def first(self):
        self.copy(2).wait_recv()
        self.make(4, self.both(2, 0))
        self.make(5, self.both(2, 1))
        self.copy(1).wait_recv()
        self.make(6, self.both(1, 0))
        self.copy(3).wait_recv()
        self.make(7, self.both(3, 1))

    def second(self):
        self.copy(4).wait_recv()
        self.make(8, self.both(3, 0) + self.land[0].astype(F32))
        self.copy(5).wait_recv()
        self.make(9, self.both(1, 1) + self.land[1].astype(F32))

    def total(self, out):
        self.copy(0).wait_recv()
        for k in (6, 7, 8, 9):
            self.copy(k).wait_recv()
        out[0:64, :] = self.both(0, 0) + self.land[2].astype(F32) + self.land[4].astype(F32)
        out[64:128, :] = self.both(0, 1) + self.land[3].astype(F32) + self.land[5].astype(F32)

    def finish(self):
        for k in range(10):
            self.copy(k).wait_send()


class Reduce:
    def __init__(self, place, grad, r1a, r1b, sa, sb, r2a, r2b, quarter, landed, final, home, send, recv):
        self.p, self.grad = place, grad
        self.r1a, self.r1b, self.sa, self.sb, self.r2a, self.r2b = r1a, r1b, sa, sb, r2a, r2b
        self.quarter, self.landed, self.final, self.home = quarter, landed, final, home
        self.send, self.recv = send, recv
        p = place
        self.near = {"xl": 1 - p.xl}
        self.cross = {"xl": 1 - p.xl, "xh": 1 - p.xh}
        odd = lax.rem(p.xl + p.xh, 2)
        self.keep = [lax.rem(odd + 1 - k, 2) for k in range(2)]

    def copy(self, k):
        p = self.p
        if k < 2:
            src, dst, device = self.grad.at[pl.ds(0, 4), k, 1 - self.keep[k]], self.r1a.at[:, k], self.near
        elif k < 4:
            src, dst, device = self.grad.at[pl.ds(4, 4), k - 2, 1 - p.xh], self.r1b.at[:, k - 2], self.cross
        elif k == 4:
            src, dst, device = self.sa, self.r2a, self.cross
        elif k == 5:
            src, dst, device = self.sb, self.r2b, self.near
        elif k < 13:
            dz = k - 5
            target = lax.rem(p.z + dz, 8)
            src, dst, device = self.quarter.at[target], self.landed.at[dz - 1], {"z": target}
        else:
            src, dst, device = self.final, self.home, p.swap
        return remote(src, dst, self.send.at[k], self.recv.at[k], device)

    def begin(self):
        for k in range(4):
            self.copy(k).start()

    def second(self):
        p = self.p
        for k in range(4):
            self.copy(k).wait_recv()
        keep = [self.grad[0:4, k, self.keep[k]].astype(F32) + self.r1a[:, k].astype(F32) for k in range(2)]
        mine = p.xl == 0
        self.sa[...] = jnp.where(mine, keep[0], keep[1]).astype(BF16)
        self.copy(4).start()
        self.quarter[0:4] = jnp.where(mine, keep[1], keep[0]).astype(BF16)
        keep = [self.grad[4:8, k, p.xh].astype(F32) + self.r1b[:, k].astype(F32) for k in range(2)]
        self.sb[...] = jnp.where(mine, keep[0], keep[1]).astype(BF16)
        self.copy(5).start()
        self.quarter[4:8] = jnp.where(mine, keep[1], keep[0]).astype(BF16)

    def third(self):
        self.copy(4).wait_recv()
        self.quarter[0:4] = (self.quarter[0:4].astype(F32) + self.r2a[...].astype(F32)).astype(BF16)
        self.copy(5).wait_recv()
        self.quarter[4:8] = (self.quarter[4:8].astype(F32) + self.r2b[...].astype(F32)).astype(BF16)
        for dz in (4, 3, 5, 2, 6, 1, 7):
            self.copy(5 + dz).start()

    def fourth(self):
        total = self.quarter[self.p.z].astype(F32)
        for dz in range(1, 8):
            self.copy(5 + dz).wait_recv()
            total = total + self.landed[dz - 1].astype(F32)
        self.final[...] = total.astype(BF16)
        self.copy(13).start()

    def finish(self):
        self.copy(13).wait_recv()
        for k in range(14):
            self.copy(k).wait_send()


INV_ROOT = 1.0 / math.sqrt(HSIZE)


def layer_kernel(
    inv_tokens,
    x_ref, dil_ref, pw_ref, cot_ref, wq_ref, wk_ref, wv_ref, wo_ref,
    out_home, home1, home2, home3,
    xall, act, taps, cpre, mid, midall, pwall, cotall, normed, dil, wqkv, wo, resid, op_part,
    q_b, k_b, v_b, att, dcat, dk_acc, dv_acc, gr, gms, gmr, gpad, moved, rows_f32, out_low,
    near, made, land, red1, red2, red3,
    swap_send, swap_recv, piece_send, piece_recv, local_sem, ag_send, ag_recv, rs_send, rs_recv, rd_send, rd_recv, gm_send, gm_recv, home_send, home_recv,
):
    p = Place()
    mine = p.block(0)
    there = p.y * 2 + p.xh
    taps[0:STEP, :] = jnp.zeros((STEP, 384), F32)
    taps[LEN + STEP :, :] = jnp.zeros((STEP, 384), F32)
    gpad[0:STEP, :] = jnp.zeros((STEP, 128), BF16)
    gpad[LEN + STEP :, :] = jnp.zeros((STEP, 128), BF16)
    for j in range(8):
        pwall[j * 128 + INNER : (j + 1) * 128, :] = jnp.zeros((32, CH), BF16)
    for k in range(3):
        dil[k * 128 + INNER : (k + 1) * 128, :] = jnp.zeros((32, CH), BF16)

    rd1 = Reduce(p, *red1, home1, rd_send.at[0], rd_recv.at[0])
    rd2 = Reduce(p, *red2, home2, rd_send.at[1], rd_recv.at[1])
    rd3 = Reduce(p, *red3, home3, rd_send.at[2], rd_recv.at[2])
    greet(
        [p.swap, rd1.near, rd1.cross, p.twin]
        + [spot(p, d, side)[1] for d in (1, 2, 3) for side in (0, 1)]
        + [{"z": lax.rem(p.z + dz, 8)} for dz in range(1, 8)]
    )

    def at(ref, block, pitch, rows):
        return ref.at[pl.ds(pl.multiple_of(block * pitch, pitch), rows)]

    def piece(ref, k, rows):
        return ref.at[pl.ds(k, rows)]

    swaps = [
        (x_ref.at[0], at(xall, there, ROWS, ROWS), at(xall, mine, ROWS, ROWS)),
        (pw_ref, at(pwall, there, 128, INNER), at(pwall, mine, 128, INNER)),
        (cot_ref.at[0], at(cotall, there, ROWS, ROWS), at(cotall, mine, ROWS, ROWS)),
    ]
    crossed = p.c != p.xh

    def swap_copy(k):
        src, dst, _ = swaps[k]
        return remote(src, dst, swap_send.at[k], swap_recv.at[k], p.swap)

    def swap_arrive(k):
        src, _, here = swaps[k]
        remote(src, here, swap_send.at[k], swap_recv.at[k], p.swap).wait_recv()

    pieces = [
        *[(dil_ref.at[k], dil, k * 128, INNER) for k in range(3)],
        *[(ref, wqkv, k * HSIZE, HSIZE) for k, ref in enumerate((wq_ref, wk_ref, wv_ref))],
        (wo_ref, wo, 0, HSIZE),
    ]

    def part_of(ref, base, rows, half):
        return ref.at[pl.ds(pl.multiple_of(base + half * (rows // 2), 16), rows // 2)]

    def piece_sent(k):
        src, dst, base, rows = pieces[k]
        half = 1 - p.xl
        return remote(part_of(src, 0, rows, half), part_of(dst, base, rows, half),
                      piece_send.at[0, k], piece_recv.at[0, k], p.swap)

    def piece_half(k, stage, half, device):
        _, dst, base, rows = pieces[k]
        ref = part_of(dst, base, rows, half)
        return remote(ref, ref, piece_send.at[stage, k], piece_recv.at[stage, k], device)

    def piece_local(k):
        src, dst, base, rows = pieces[k]
        return pltpu.make_async_copy(src, piece(dst, base, rows), local_sem.at[k])

    def piece_pass(*ks):
        @pl.when(crossed)
        def _():
            for k in ks:
                piece_half(k, 0, p.xl, p.swap).wait_recv()
                piece_half(k, 1, p.xl, rd1.near).start()

    def piece_arrive(*ks):
        @pl.when(crossed)
        def _():
            for k in ks:
                piece_half(k, 1, 1 - p.xl, rd1.near).wait_recv()

        @pl.when(jnp.logical_not(crossed))
        def _():
            for k in ks:
                piece_local(k).wait()

    pw_local = pltpu.make_async_copy(pw_ref, at(pwall, mine, 128, INNER), local_sem.at[7])

    ag_x = Gather(p, row_view(xall, ROWS, ROWS), ag_send.at[0], ag_recv.at[0])
    ag_pw = Gather(p, row_view(pwall, 128, INNER), ag_send.at[1], ag_recv.at[1])
    ag_mid = Gather(p, column_view(midall), ag_send.at[2], ag_recv.at[2])
    ag_cot = Gather(p, row_view(cotall, ROWS, ROWS), ag_send.at[3], ag_recv.at[3])
    ag_gr = Gather(p, row_view(gr, ROWS, ROWS), ag_send.at[4], ag_recv.at[4])

    def pair_rows(d):
        return pl.multiple_of(lax.rem(p.y + d, 4) * 256, 256)

    def activate(d):
        base = pair_rows(d)

        @pl.loop(0, 8)
        def _(i):
            rows = pl.ds(pl.multiple_of(base + i * 32, 32), 32)
            value = xall[rows, :].astype(F32)
            act[rows, :] = jax.nn.gelu(value * rms_scale(value)).astype(BF16)

    def tap(d):
        base = pair_rows(d)
        taps[pl.ds(base + STEP, 256), :] = dot_nt(act[pl.ds(base, 256), :], dil[...])

    swap_copy(0).start()

    @pl.when(crossed)
    def _():
        for k in range(3):
            piece_sent(k).start()
        swap_copy(1).start()

    swap_copy(2).start()

    @pl.when(crossed)
    def _():
        for k in range(3, 7):
            piece_sent(k).start()

    @pl.when(jnp.logical_not(crossed))
    def _():
        pw_local.start()
        for k in range(7):
            piece_local(k).start()
        pw_local.wait()
        ag_pw.begin()
        ag_pw.forward()

    swap_arrive(0)
    ag_x.begin()
    ag_x.arrive(6)
    activate(0)
    ag_x.forward()
    piece_pass(0, 1, 2)
    ag_x.share()
    piece_arrive(0, 1, 2)
    tap(0)
    ag_x.arrive(7)
    activate(3)
    tap(3)
    ag_x.share_far()

    @pl.when(crossed)
    def _():
        swap_arrive(1)
        ag_pw.begin()

    ag_x.arrive(8)
    activate(1)
    tap(1)

    @pl.when(crossed)
    def _():
        ag_pw.forward()

    ag_x.arrive(9)
    activate(2)
    tap(2)

    @pl.loop(0, 8)
    def _(i):
        base = pl.multiple_of(i * 128, 128)
        total = (
            taps[pl.ds(base, 128), 0:128]
            + taps[pl.ds(base + STEP, 128), 128:256]
            + taps[pl.ds(base + 2 * STEP, 128), 256:384]
        )
        cpre[pl.ds(base, 128), :] = total
        low = jax.nn.gelu(total).astype(BF16)
        mid[pl.ds(base, 128), :] = low
        midall[pl.ds(base, 128), pl.ds(pl.multiple_of(mine * 128, 128), 128)] = low

    ag_mid.begin()
    ag_pw.share()
    ag_pw.share_far()
    ag_mid.forward()
    swap_arrive(2)
    ag_cot.begin()
    piece_pass(3, 4, 5, 6)
    ag_mid.share()
    ag_mid.share_far()
    ag_pw.arrive(6, 7, 8, 9)
    ag_mid.arrive(6, 7, 8, 9)

    @pl.loop(0, 4)
    def _(i):
        rows = pl.ds(pl.multiple_of(i * 256, 256), 256)
        total = xall[rows, :].astype(F32) + dot_nn(midall[rows, :], pwall[...])
        low = total.astype(BF16)
        wide = low.astype(F32)
        normed[rows, :] = (wide * rms_scale(wide)).astype(BF16)

        @pl.when(i == p.y)
        def _():
            resid[...] = jnp.where(p.c == 0, low[0:128], low[128:256])

    ag_cot.forward()
    piece_arrive(3, 4, 5)

    @pl.loop(0, 4)
    def _(i):
        rows = pl.ds(pl.multiple_of(i * 256, 256), 256)
        tile = normed[rows, :]
        q_b[rows, :] = dot_nt(tile, wqkv[0:HSIZE, :]).astype(BF16)
        k_b[rows, :] = dot_nt(tile, wqkv[HSIZE : 2 * HSIZE, :]).astype(BF16)
        v_b[rows, :] = dot_nt(tile, wqkv[2 * HSIZE :, :]).astype(BF16)

    ag_cot.share()
    piece_arrive(6)
    dk_acc[...] = jnp.zeros_like(dk_acc)
    dv_acc[...] = jnp.zeros_like(dv_acc)

    def attend(d):
        rows = pl.ds(pair_rows(d), 256)
        gh_tile = (dot_nt(cotall[rows, :], wo[...]) * inv_tokens).astype(BF16)
        q_tile = q_b[rows, :]
        ratio = jnp.tanh(dot_nt(q_tile, k_b[...]) * (INV_ROOT / SOFT_CAP))
        unnormed = jnp.exp(SOFT_CAP * ratio)
        weights = unnormed / jnp.sum(unnormed, axis=-1, keepdims=True)
        weights_low = weights.astype(BF16)
        att[rows, :] = dot_nn(weights_low, v_b[...]).astype(BF16)
        dv_acc[...] += dot_tn(weights_low, gh_tile)
        grad_soft = dot_nt(gh_tile, v_b[...])
        grad_capped = weights * (grad_soft - jnp.sum(weights * grad_soft, axis=-1, keepdims=True))
        score = (grad_capped * (1.0 - ratio * ratio)).astype(BF16)
        dcat[rows, 0:HSIZE] = (dot_nn(score, k_b[...]) * INV_ROOT).astype(BF16)
        dk_acc[...] += dot_tn(score, q_tile)

    ag_cot.arrive(6)
    attend(0)
    ag_cot.arrive(7)
    attend(3)
    ag_cot.share_far()
    ag_cot.arrive(8)
    attend(1)
    ag_cot.arrive(9)
    attend(2)
    ag_x.finish()
    dcat[:, HSIZE : 2 * HSIZE] = (dk_acc[...] * INV_ROOT).astype(BF16)
    dcat[:, 2 * HSIZE :] = dv_acc[...].astype(BF16)

    gn_part = xall
    rs_gn = Scatter(p, gn_part, near.at[0], made.at[0], land.at[0], rs_send.at[0], rs_recv.at[0])
    rs_op = Scatter(p, op_part, near.at[1], made.at[1], land.at[1], rs_send.at[1], rs_recv.at[1])
    for d in (2, 1, 3, 0):
        rows = pl.ds(pair_rows(d), 256)
        gn_part[rows, :] = dot_nn(dcat[rows, :], wqkv[...]).astype(BF16)
        rs_gn.copy(d).start()
    rs_gn.first()
    grad1, grad2, grad3 = red1[0], red2[0], red3[0]

    @pl.loop(0, 4)
    def _(i):
        columns = pl.ds(pl.multiple_of(i * 384, 384), 384)
        value = dot_tn(normed[:, columns], dcat[...]).astype(BF16)
        grad1[pl.ds(2 * i, 2), :, :, :, 0:576] = value.reshape(2, 2, 2, 48, 576)
        value = (dot_tn(cotall[:, columns], att[...]) * inv_tokens).astype(BF16)
        grad1[pl.ds(2 * i, 2), :, :, :, 576:768] = value.reshape(2, 2, 2, 48, HSIZE)

    rd1.begin()
    for d in (2, 1, 3, 0):
        rows = pl.ds(pair_rows(d), 256)
        op_part[rows, :] = dot_nn(att[rows, :], wo[...]).astype(BF16)
        rs_op.copy(d).start()
    rs_gn.second()
    rs_gn.total(rows_f32)

    own = pl.multiple_of(mine * ROWS, ROWS)

    @pl.loop(0, 4)
    def _(i):
        rows = pl.ds(pl.multiple_of(i * 32, 32), 32)
        total = rows_f32[rows, :]
        wide = resid[rows, :].astype(F32)
        scale = rms_scale(wide)
        gr[pl.ds(own + i * 32, 32), :] = (
            cotall[pl.ds(own + i * 32, 32), :].astype(F32) * inv_tokens
            + scale * total
            - wide * scale**3 * jnp.mean(total * wide, axis=-1, keepdims=True)
        ).astype(BF16)

    gm_value = dot_nt(gr[pl.ds(own, ROWS), :], pwall[...]).astype(BF16)
    for j in range(8):
        gms[j, :, :] = gm_value[:, j * 128 : (j + 1) * 128]
    spots = [(d, side) for d in (2, 1, 3, 0) for side in (0, 1) if (d, side) != (0, 0)]

    def gm_copy(k):
        block, device = spot(p, *spots[k])
        return remote(gms.at[block], gmr.at[pl.ds(own, ROWS)], gm_send.at[k], gm_recv.at[k], device)

    def gm_arrive(k):
        d, side = spots[k]
        block, device = spot(p, (4 - d) % 4, side)
        here = gmr.at[pl.ds(pl.multiple_of(block * ROWS, ROWS), ROWS)]
        remote(gms.at[0], here, gm_send.at[k], gm_recv.at[k], device).wait_recv()

    for k in range(7):
        gm_copy(k).start()
    ag_gr.begin()
    gmr[pl.ds(own, ROWS), :] = gms[mine]
    rd1.second()
    for k in range(7):
        gm_arrive(k)

    @pl.loop(0, 8)
    def _(i):
        rows = pl.ds(pl.multiple_of(i * 128, 128), 128)
        value = gelu_back(cpre[rows, :], gmr[rows, :].astype(F32))
        gpad[pl.ds(pl.multiple_of(i * 128 + STEP, STEP), 128), :] = value.astype(BF16)

    moved[:, 0:INNER] = gpad[2 * STEP :, 0:INNER]
    moved[:, INNER : 2 * INNER] = gpad[STEP : LEN + STEP, 0:INNER]
    moved[:, 2 * INNER :] = gpad[0:LEN, 0:INNER]

    @pl.loop(0, 4)
    def _(i):
        columns = pl.ds(pl.multiple_of(i * 384, 384), 384)
        value = dot_tn(act[:, columns], moved[...]).astype(BF16)
        grad2[pl.ds(2 * i, 2)] = value[:, 0:256].reshape(2, 2, 2, 48, 256)
        grad3[pl.ds(2 * i, 2), :, :, :, INNER:128] = value[:, 256:].reshape(2, 2, 2, 48, 32)

    rd2.begin()
    ag_gr.forward()
    rs_op.first()
    ag_gr.share()
    rd1.third()
    ag_gr.share_far()
    rd2.second()
    ag_gr.arrive(6, 7, 8, 9)

    @pl.loop(0, 4)
    def _(i):
        columns = pl.ds(pl.multiple_of(i * 384, 384), 384)
        value = dot_tn(gr[:, columns], mid[...]).astype(BF16)
        grad3[pl.ds(2 * i, 2), :, :, :, 0:INNER] = value[:, 0:INNER].reshape(2, 2, 2, 48, INNER)

    rd3.begin()
    rd2.third()
    rs_op.second()
    rs_op.total(rows_f32)
    out_low[...] = (resid[...].astype(F32) + rows_f32[...]).astype(BF16)
    rd3.second()
    home = remote(out_low, out_home, home_send, home_recv, p.swap)
    home.start()
    rd3.third()
    rd1.fourth()
    rd2.fourth()
    rd3.fourth()
    for rd in (rd1, rd2, rd3):
        rd.finish()
    home.wait_recv()
    home.wait_send()
    swap_copy(0).wait_send()
    swap_copy(2).wait_send()

    @pl.when(crossed)
    def _():
        swap_copy(1).wait_send()
        for k in range(7):
            piece_sent(k).wait_send()
            piece_half(k, 1, p.xl, rd1.near).wait_send()

    for k in range(7):
        gm_copy(k).wait_send()
    for part in (rs_gn, rs_op, ag_pw, ag_mid, ag_cot, ag_gr):
        part.finish()


def shape(*dims, dtype=BF16):
    return jax.ShapeDtypeStruct(dims, dtype)


def reduce_scratch(width):
    half = pltpu.VMEM((4, 2, 48, width), BF16)
    part = pltpu.VMEM((4, 48, width), BF16)
    return (
        pltpu.VMEM((8, 2, 2, 48, width), BF16), half, half, part, part, part, part,
        pltpu.VMEM((8, 48, width), BF16), pltpu.VMEM((7, 48, width), BF16), pltpu.VMEM((48, width), BF16),
    )


def layer(inv_tokens, x, dil, pw, cot, wq, wk, wv, wo):
    whole = pltpu.VMEM((LEN, CH), BF16)
    head = pltpu.VMEM((LEN, HSIZE), BF16)
    dma = pltpu.SemaphoreType.DMA
    return pl.pallas_call(
        functools.partial(layer_kernel, inv_tokens),
        name="layer",
        out_shape=(shape(ROWS, CH), shape(48, 768), shape(48, 256), shape(48, 128)),
        in_specs=[ANY_SPEC] * 8,
        out_specs=(VMEM_SPEC,) * 4,
        scratch_shapes=[
            whole, whole,
            pltpu.VMEM((LEN + 2 * STEP, 384), F32),
            pltpu.VMEM((LEN, 128), F32),
            pltpu.VMEM((LEN, 128), BF16),
            pltpu.VMEM((LEN, 1024), BF16),
            pltpu.VMEM((1024, CH), BF16),
            whole, whole,
            pltpu.VMEM((384, CH), BF16),
            pltpu.VMEM((3 * HSIZE, CH), BF16),
            pltpu.VMEM((HSIZE, CH), BF16),
            pltpu.VMEM((ROWS, CH), BF16),
            whole,
            head, head, head, head,
            pltpu.VMEM((LEN, 3 * HSIZE), BF16),
            pltpu.VMEM((LEN, HSIZE), F32),
            pltpu.VMEM((LEN, HSIZE), F32),
            whole,
            pltpu.VMEM((8, 128, 128), BF16),
            pltpu.VMEM((LEN, 128), BF16),
            pltpu.VMEM((LEN + 2 * STEP, 128), BF16),
            pltpu.VMEM((LEN, 3 * INNER), BF16),
            pltpu.VMEM((ROWS, CH), F32),
            pltpu.VMEM((ROWS, CH), BF16),
            pltpu.VMEM((2, 4, ROWS, CH), BF16),
            pltpu.VMEM((2, 6, 64, CH), BF16),
            pltpu.VMEM((2, 6, 64, CH), BF16),
            reduce_scratch(768),
            reduce_scratch(256),
            reduce_scratch(128),
            dma((3,)), dma((3,)), dma((2, 7)), dma((2, 7)), dma((8,)), dma((5, 10)), dma((5, 10)), dma((2, 10)), dma((2, 10)),
            dma((3, 14)), dma((3, 14)), dma((7,)), dma((7,)), dma, dma,
        ],
        compiler_params=pltpu.CompilerParams(
            collective_id=0, has_side_effects=True, vmem_limit_bytes=LIMIT
        ),
    )(x, dil, pw, cot, wq, wk, wv, wo)


def split_kernel(low, h1, h2, h3, output, gd, gp, gq, gk, gv, go):
    output[0] = low[...]
    wide = h1[...].astype(F32)
    gq[...] = wide[:, 0:HSIZE]
    gk[...] = wide[:, HSIZE : 2 * HSIZE]
    gv[...] = wide[:, 2 * HSIZE : 3 * HSIZE]
    go[...] = wide[:, 3 * HSIZE :]
    taps = h2[...].astype(F32)
    rest = h3[...].astype(F32)
    gd[0] = taps[:, 0:INNER]
    gd[1] = taps[:, INNER : 2 * INNER]
    gd[2, :, 0:64] = taps[:, 2 * INNER :]
    gd[2, :, 64:INNER] = rest[:, INNER:]
    gp[...] = rest[:, 0:INNER]


def shards(x, dil, pw, wq, wk, wv, wo, cot):
    inv_tokens = 1.0 / math.sqrt(BATCH * LEN)
    homes = layer(inv_tokens, x, dil, pw, cot, wq, wk, wv, wo)
    square = shape(48, HSIZE, dtype=F32)
    output, gd, gp, gq, gk, gv, go = pl.pallas_call(
        split_kernel,
        name="split",
        out_shape=(
            shape(1, ROWS, CH), shape(3, 48, INNER, dtype=F32), shape(48, INNER, dtype=F32),
            square, square, square, square,
        ),
        in_specs=[VMEM_SPEC] * 4,
        out_specs=(VMEM_SPEC,) * 7,
    )(*homes)
    return (output, gd, gp.T, gq, gk, gv, go.T)


def solution(mesh):
    torus = Mesh(mesh.devices.reshape(8, 2, 2, 4, 2), AXES)
    in_specs = (
        P(DP, SEQ, None),
        P(None, SEQ, None),
        P(SEQ, None),
        P(SEQ, None),
        P(SEQ, None),
        P(SEQ, None),
        P(SEQ, None),
        P(DP, SEQ, None),
    )
    out_specs = (
        P(DP, SEQ, None),
        P(None, DP, SEQ),
        P(SEQ, DP),
        P(DP, SEQ),
        P(DP, SEQ),
        P(DP, SEQ),
        P(SEQ, DP),
    )
    return jax.shard_map(
        shards, mesh=torus, in_specs=in_specs, out_specs=out_specs, check_vma=False
    )
```

```python
import functools
import math

import jax
import jax.numpy as jnp
from jax import lax
from jax.experimental import pallas as pl
from jax.experimental.pallas import tpu as pltpu
from jax.sharding import Mesh
from jax.sharding import PartitionSpec as P

HSIZE = 192
STEP = 16
EPSILON = 1e-06
SOFT_CAP = 6.0
LEN = 1024
CH = 1536
INNER = 96
ROWS = 128
BATCH = 32
AXES = ("z", "xl", "c", "y", "xh")
DP = ("z", "xl", "c")
SEQ = ("y", "xh")
MESH_ID = pl.DeviceIdType.MESH
F32 = jnp.float32
BF16 = jnp.bfloat16
VMEM_SPEC = pl.BlockSpec(memory_space=pltpu.VMEM)
ANY_SPEC = pl.BlockSpec(memory_space=pl.ANY)
LIMIT = 62 * 1024 * 1024


def dot_nt(a, b):
    return lax.dot_general(a, b, (((1,), (1,)), ((), ())), preferred_element_type=F32)


def dot_nn(a, b):
    return jnp.dot(a, b, preferred_element_type=F32)


def dot_tn(a, b):
    return lax.dot_general(a, b, (((0,), (0,)), ((), ())), preferred_element_type=F32)


def rms_scale(rows):
    return lax.rsqrt(jnp.mean(rows * rows, axis=-1, keepdims=True) + EPSILON)


def gelu_back(pre_act, upstream):
    return jax.vjp(jax.nn.gelu, pre_act)[1](upstream)[0]


class Place:
    def __init__(self):
        self.z = lax.axis_index("z")
        self.xl = lax.axis_index("xl")
        self.c = lax.axis_index("c")
        self.y = lax.axis_index("y")
        self.xh = lax.axis_index("xh")
        self.up = {"y": lax.rem(self.y + 1, 4)}
        self.down = {"y": lax.rem(self.y + 3, 4)}
        self.twin = {"c": 1 - self.c}
        self.swap = {"xl": 1 - self.xl, "xh": self.c, "c": self.xh}

    def block(self, d, mine=True):
        return lax.rem(self.y + d, 4) * 2 + (self.c if mine else 1 - self.c)


def greet(devices):
    barrier = pltpu.get_barrier_semaphore()
    for device in devices:
        pl.semaphore_signal(barrier, inc=1, device_id=device, device_id_type=MESH_ID)
    pl.semaphore_wait(barrier, len(devices))


def remote(src, dst, send, recv, device):
    return pltpu.make_async_remote_copy(
        src_ref=src, dst_ref=dst, send_sem=send, recv_sem=recv,
        device_id=device, device_id_type=MESH_ID,
    )


class Gather:
    def __init__(self, place, view, send, recv):
        self.view, self.send, self.recv = view, send, recv
        p = place
        own, low, high, far = (p.block(d) for d in (0, 3, 1, 2))
        own2, low2, high2, far2 = (p.block(d, False) for d in (0, 3, 1, 2))
        self.out = [
            (own, 0, p.up), (own, 1, p.up), (low, 0, p.up),
            (own, 1, p.down), (own, 0, p.down), (high, 1, p.down),
            (own, None, p.twin), (low, None, p.twin), (high, None, p.twin), (far, None, p.twin),
        ]
        self.inn = [
            (low, 0), (low, 1), (far, 0), (high, 1), (high, 0), (far, 1),
            (own2, None), (low2, None), (high2, None), (far2, None),
        ]

    def copy(self, k):
        block, half, device = self.out[k]
        ref = self.view(block, half)
        return remote(ref, ref, self.send.at[k], self.recv.at[k], device)

    def start(self, *ks):
        for k in ks:
            self.copy(k).start()

    def arrive(self, *ks):
        for k in ks:
            block, half = self.inn[k]
            ref = self.view(block, half)
            remote(ref, ref, self.send.at[k], self.recv.at[k], self.out[k][2]).wait_recv()

    def begin(self):
        self.start(0, 3, 1, 4, 6)

    def forward(self):
        self.arrive(0)
        self.start(2)
        self.arrive(3)
        self.start(5)

    def share(self):
        self.arrive(1)
        self.start(7)
        self.arrive(4)
        self.start(8)

    def share_far(self):
        self.arrive(2, 5)
        self.start(9)

    def finish(self):
        for k in range(10):
            self.copy(k).wait_send()


def row_view(ref, pitch, rows):
    def view(block, half):
        if half is None:
            return ref.at[pl.ds(pl.multiple_of(block * pitch, pitch), rows)]
        start = pl.multiple_of(block * pitch + half * (rows // 2), 16)
        return ref.at[pl.ds(start, rows // 2)]
    return view


def column_view(ref):
    def view(block, half):
        columns = pl.ds(pl.multiple_of(block * 128, 128), 128)
        if half is None:
            return ref.at[:, columns]
        return ref.at[pl.ds(half * (LEN // 2), LEN // 2), columns]
    return view


def spot(p, d, side):
    core = p.c if side == 0 else 1 - p.c
    y = lax.rem(p.y + d, 4)
    return y * 2 + core, ({"y": y} if side == 0 else {"y": y, "c": core})


class Scatter:
    def __init__(self, place, part, near, made, land, send, recv):
        self.p, self.part, self.near, self.made, self.land = place, part, near, made, land
        self.send, self.recv = send, recv

    def own_rows(self, d, half):
        start = pl.multiple_of(self.p.block(d) * ROWS + half * 64, 64)
        return self.part[pl.ds(start, 64), :].astype(F32)

    def both(self, d, half):
        rows = slice(half * 64, half * 64 + 64)
        return self.own_rows(d, half) + self.near[d, rows, :].astype(F32)

    def copies(self, k):
        p = self.p
        if k < 4:
            start = pl.multiple_of(p.block(k, False) * ROWS, ROWS)
            return self.part.at[pl.ds(start, ROWS)], self.near.at[k], p.twin
        d, half, device = [
            (2, 0, p.down), (2, 1, p.up), (1, 0, p.up), (3, 1, p.down), (3, 0, p.down), (1, 1, p.up)
        ][k - 4]
        return self.made.at[k - 4], self.land.at[k - 4], device

    def copy(self, k):
        src, dst, device = self.copies(k)
        return remote(src, dst, self.send.at[k], self.recv.at[k], device)

    def begin(self):
        for d in (2, 1, 3, 0):
            self.copy(d).start()

    def make(self, k, value):
        self.made[k - 4, :, :] = value.astype(BF16)
        self.copy(k).start()

    def direct(self):
        self.copy(1).wait_recv()
        self.make(6, self.both(1, 0))
        self.copy(3).wait_recv()
        self.make(7, self.both(3, 1))

    def far(self):
        self.copy(2).wait_recv()
        self.make(4, self.both(2, 0))
        self.make(5, self.both(2, 1))

    def second(self):
        self.copy(4).wait_recv()
        self.make(8, self.both(3, 0) + self.land[0].astype(F32))
        self.copy(5).wait_recv()
        self.make(9, self.both(1, 1) + self.land[1].astype(F32))

    def total(self, out):
        self.copy(0).wait_recv()
        for k in (6, 7, 8, 9):
            self.copy(k).wait_recv()
        out[0:64, :] = self.both(0, 0) + self.land[2].astype(F32) + self.land[4].astype(F32)
        out[64:128, :] = self.both(0, 1) + self.land[3].astype(F32) + self.land[5].astype(F32)

    def finish(self):
        for k in range(10):
            self.copy(k).wait_send()


class Reduce:
    def __init__(self, place, grad, r1a, r1b, sa, sb, r2a, r2b, quarter, landed, final, home, send, recv):
        self.p, self.grad = place, grad
        self.r1a, self.r1b, self.sa, self.sb, self.r2a, self.r2b = r1a, r1b, sa, sb, r2a, r2b
        self.quarter, self.landed, self.final, self.home = quarter, landed, final, home
        self.send, self.recv = send, recv
        p = place
        self.near = {"xl": 1 - p.xl}
        self.cross = {"xl": 1 - p.xl, "xh": 1 - p.xh}
        odd = lax.rem(p.xl + p.xh, 2)
        self.keep = [lax.rem(odd + 1 - k, 2) for k in range(2)]

    def copy(self, k):
        p = self.p
        if k < 2:
            src, dst, device = self.grad.at[pl.ds(0, 4), k, 1 - self.keep[k]], self.r1a.at[:, k], self.near
        elif k < 4:
            src, dst, device = self.grad.at[pl.ds(4, 4), k - 2, 1 - p.xh], self.r1b.at[:, k - 2], self.cross
        elif k == 4:
            src, dst, device = self.sa, self.r2a, self.cross
        elif k == 5:
            src, dst, device = self.sb, self.r2b, self.near
        elif k < 13:
            dz = k - 5
            target = lax.rem(p.z + dz, 8)
            src, dst, device = self.quarter.at[target], self.landed.at[dz - 1], {"z": target}
        else:
            src, dst, device = self.final, self.home, p.swap
        return remote(src, dst, self.send.at[k], self.recv.at[k], device)

    def begin(self):
        for k in range(4):
            self.copy(k).start()

    def second(self):
        p = self.p
        for k in range(4):
            self.copy(k).wait_recv()
        keep = [self.grad[0:4, k, self.keep[k]].astype(F32) + self.r1a[:, k].astype(F32) for k in range(2)]
        mine = p.xl == 0
        self.sa[...] = jnp.where(mine, keep[0], keep[1]).astype(BF16)
        self.copy(4).start()
        self.quarter[0:4] = jnp.where(mine, keep[1], keep[0]).astype(BF16)
        keep = [self.grad[4:8, k, p.xh].astype(F32) + self.r1b[:, k].astype(F32) for k in range(2)]
        self.sb[...] = jnp.where(mine, keep[0], keep[1]).astype(BF16)
        self.copy(5).start()
        self.quarter[4:8] = jnp.where(mine, keep[1], keep[0]).astype(BF16)

    def third(self):
        self.copy(4).wait_recv()
        self.quarter[0:4] = (self.quarter[0:4].astype(F32) + self.r2a[...].astype(F32)).astype(BF16)
        self.copy(5).wait_recv()
        self.quarter[4:8] = (self.quarter[4:8].astype(F32) + self.r2b[...].astype(F32)).astype(BF16)
        for dz in (4, 3, 5, 2, 6, 1, 7):
            self.copy(5 + dz).start()

    def fourth(self):
        total = self.quarter[self.p.z].astype(F32)
        for dz in range(1, 8):
            self.copy(5 + dz).wait_recv()
            total = total + self.landed[dz - 1].astype(F32)
        self.final[...] = total.astype(BF16)
        self.copy(13).start()

    def finish(self):
        self.copy(13).wait_recv()
        for k in range(14):
            self.copy(k).wait_send()


INV_ROOT = 1.0 / math.sqrt(HSIZE)


def layer_kernel(
    inv_tokens,
    x_ref, dil_ref, pw_ref, cot_ref, wq_ref, wk_ref, wv_ref, wo_ref,
    out_home, home1, home2, home3,
    xall, act, taps, cpre, mid, midall, pwall, cotall, normed, dil, wqkv, wo, resid, op_part,
    q_b, k_b, v_b, att, dcat, dk_acc, dv_acc, gr, gms, gmr, gpad, moved, rows_f32, out_low,
    near, made, land, red1, red2, red3,
    swap_send, swap_recv, piece_send, piece_recv, local_sem, ag_send, ag_recv, rs_send, rs_recv, rd_send, rd_recv, gm_send, gm_recv, home_send, home_recv,
):
    p = Place()
    mine = p.block(0)
    there = p.y * 2 + p.xh
    taps[0:STEP, :] = jnp.zeros((STEP, 384), F32)
    taps[LEN + STEP :, :] = jnp.zeros((STEP, 384), F32)
    gpad[0:STEP, :] = jnp.zeros((STEP, 128), BF16)
    gpad[LEN + STEP :, :] = jnp.zeros((STEP, 128), BF16)
    for j in range(8):
        pwall[j * 128 + INNER : (j + 1) * 128, :] = jnp.zeros((32, CH), BF16)
    for k in range(3):
        dil[k * 128 + INNER : (k + 1) * 128, :] = jnp.zeros((32, CH), BF16)

    rd1 = Reduce(p, *red1, home1, rd_send.at[0], rd_recv.at[0])
    rd2 = Reduce(p, *red2, home2, rd_send.at[1], rd_recv.at[1])
    rd3 = Reduce(p, *red3, home3, rd_send.at[2], rd_recv.at[2])
    greet(
        [p.swap, rd1.near, rd1.cross, p.twin]
        + [spot(p, d, side)[1] for d in (1, 2, 3) for side in (0, 1)]
        + [{"z": lax.rem(p.z + dz, 8)} for dz in range(1, 8)]
    )

    def at(ref, block, pitch, rows):
        return ref.at[pl.ds(pl.multiple_of(block * pitch, pitch), rows)]

    def piece(ref, k, rows):
        return ref.at[pl.ds(k, rows)]

    swaps = [
        (x_ref.at[0], at(xall, there, ROWS, ROWS), at(xall, mine, ROWS, ROWS)),
        (pw_ref, at(pwall, there, 128, INNER), at(pwall, mine, 128, INNER)),
        (cot_ref.at[0], at(cotall, there, ROWS, ROWS), at(cotall, mine, ROWS, ROWS)),
    ]
    crossed = p.c != p.xh

    def swap_copy(k):
        src, dst, _ = swaps[k]
        return remote(src, dst, swap_send.at[k], swap_recv.at[k], p.swap)

    def swap_arrive(k):
        src, _, here = swaps[k]
        remote(src, here, swap_send.at[k], swap_recv.at[k], p.swap).wait_recv()

    pieces = [
        *[(dil_ref.at[k], dil, k * 128, INNER) for k in range(3)],
        *[(ref, wqkv, k * HSIZE, HSIZE) for k, ref in enumerate((wq_ref, wk_ref, wv_ref))],
        (wo_ref, wo, 0, HSIZE),
    ]

    def part_of(ref, base, rows, half):
        return ref.at[pl.ds(pl.multiple_of(base + half * (rows // 2), 16), rows // 2)]

    def piece_sent(k):
        src, dst, base, rows = pieces[k]
        half = 1 - p.xl
        return remote(part_of(src, 0, rows, half), part_of(dst, base, rows, half),
                      piece_send.at[0, k], piece_recv.at[0, k], p.swap)

    def piece_half(k, stage, half, device):
        _, dst, base, rows = pieces[k]
        ref = part_of(dst, base, rows, half)
        return remote(ref, ref, piece_send.at[stage, k], piece_recv.at[stage, k], device)

    def piece_local(k):
        src, dst, base, rows = pieces[k]
        return pltpu.make_async_copy(src, piece(dst, base, rows), local_sem.at[k])

    def piece_pass(*ks):
        @pl.when(crossed)
        def _():
            for k in ks:
                piece_half(k, 0, p.xl, p.swap).wait_recv()
                piece_half(k, 1, p.xl, rd1.near).start()

    def piece_arrive(*ks):
        @pl.when(crossed)
        def _():
            for k in ks:
                piece_half(k, 1, 1 - p.xl, rd1.near).wait_recv()

        @pl.when(jnp.logical_not(crossed))
        def _():
            for k in ks:
                piece_local(k).wait()

    pw_local = pltpu.make_async_copy(pw_ref, at(pwall, mine, 128, INNER), local_sem.at[7])

    ag_x = Gather(p, row_view(xall, ROWS, ROWS), ag_send.at[0], ag_recv.at[0])
    ag_pw = Gather(p, row_view(pwall, 128, INNER), ag_send.at[1], ag_recv.at[1])
    ag_mid = Gather(p, column_view(midall), ag_send.at[2], ag_recv.at[2])
    ag_cot = Gather(p, row_view(cotall, ROWS, ROWS), ag_send.at[3], ag_recv.at[3])
    ag_gr = Gather(p, row_view(gr, ROWS, ROWS), ag_send.at[4], ag_recv.at[4])

    def pair_rows(d):
        return pl.multiple_of(lax.rem(p.y + d, 4) * 256, 256)

    def activate(d):
        base = pair_rows(d)

        @pl.loop(0, 8)
        def _(i):
            rows = pl.ds(pl.multiple_of(base + i * 32, 32), 32)
            value = xall[rows, :].astype(F32)
            act[rows, :] = jax.nn.gelu(value * rms_scale(value)).astype(BF16)

    def tap(d):
        base = pair_rows(d)
        taps[pl.ds(base + STEP, 256), :] = dot_nt(act[pl.ds(base, 256), :], dil[...])

    swap_copy(0).start()

    @pl.when(crossed)
    def _():
        for k in range(3):
            piece_sent(k).start()
        swap_copy(1).start()

    swap_copy(2).start()

    @pl.when(crossed)
    def _():
        for k in range(3, 7):
            piece_sent(k).start()

    @pl.when(jnp.logical_not(crossed))
    def _():
        pw_local.start()
        for k in range(7):
            piece_local(k).start()
        pw_local.wait()
        ag_pw.begin()
        ag_pw.forward()

    swap_arrive(0)
    ag_x.begin()
    ag_x.arrive(6)
    activate(0)
    ag_x.forward()
    piece_pass(0, 1, 2)
    ag_x.share()
    piece_arrive(0, 1, 2)
    tap(0)
    ag_x.arrive(7)
    activate(3)
    tap(3)
    ag_x.share_far()

    @pl.when(crossed)
    def _():
        swap_arrive(1)
        ag_pw.begin()

    ag_x.arrive(8)
    activate(1)
    tap(1)

    @pl.when(crossed)
    def _():
        ag_pw.forward()

    ag_x.arrive(9)
    activate(2)
    tap(2)

    @pl.loop(0, 8)
    def _(i):
        base = pl.multiple_of(i * 128, 128)
        total = (
            taps[pl.ds(base, 128), 0:128]
            + taps[pl.ds(base + STEP, 128), 128:256]
            + taps[pl.ds(base + 2 * STEP, 128), 256:384]
        )
        cpre[pl.ds(base, 128), :] = total
        low = jax.nn.gelu(total).astype(BF16)
        mid[pl.ds(base, 128), :] = low
        midall[pl.ds(base, 128), pl.ds(pl.multiple_of(mine * 128, 128), 128)] = low

    ag_mid.begin()
    ag_pw.share()
    ag_pw.share_far()
    ag_mid.forward()
    swap_arrive(2)
    ag_cot.begin()
    piece_pass(3, 4, 5, 6)
    ag_mid.share()
    ag_mid.share_far()
    ag_pw.arrive(6, 7, 8, 9)
    ag_mid.arrive(6, 7, 8, 9)

    @pl.loop(0, 4)
    def _(i):
        rows = pl.ds(pl.multiple_of(i * 256, 256), 256)
        total = xall[rows, :].astype(F32) + dot_nn(midall[rows, :], pwall[...])
        low = total.astype(BF16)
        wide = low.astype(F32)
        normed[rows, :] = (wide * rms_scale(wide)).astype(BF16)

        @pl.when(i == p.y)
        def _():
            resid[...] = jnp.where(p.c == 0, low[0:128], low[128:256])

    ag_cot.forward()
    piece_arrive(3, 4, 5)

    @pl.loop(0, 4)
    def _(i):
        rows = pl.ds(pl.multiple_of(i * 256, 256), 256)
        tile = normed[rows, :]
        q_b[rows, :] = dot_nt(tile, wqkv[0:HSIZE, :]).astype(BF16)
        k_b[rows, :] = dot_nt(tile, wqkv[HSIZE : 2 * HSIZE, :]).astype(BF16)
        v_b[rows, :] = dot_nt(tile, wqkv[2 * HSIZE :, :]).astype(BF16)

    ag_cot.share()
    piece_arrive(6)
    dk_acc[...] = jnp.zeros_like(dk_acc)
    dv_acc[...] = jnp.zeros_like(dv_acc)

    def attend(d):
        rows = pl.ds(pair_rows(d), 256)
        gh_tile = (dot_nt(cotall[rows, :], wo[...]) * inv_tokens).astype(BF16)
        q_tile = q_b[rows, :]
        ratio = jnp.tanh(dot_nt(q_tile, k_b[...]) * (INV_ROOT / SOFT_CAP))
        unnormed = jnp.exp(SOFT_CAP * ratio)
        weights = unnormed * (1.0 / jnp.sum(unnormed, axis=-1, keepdims=True))
        weights_low = weights.astype(BF16)
        attended = dot_nn(weights_low, v_b[...])
        att[rows, :] = attended.astype(BF16)
        dv_acc[...] += dot_tn(weights_low, gh_tile)
        grad_soft = dot_nt(gh_tile, v_b[...])
        mean_grad = jnp.sum(gh_tile.astype(F32) * attended, axis=-1, keepdims=True)
        grad_capped = weights * (grad_soft - mean_grad)
        score = (grad_capped * (1.0 - ratio * ratio)).astype(BF16)
        dcat[rows, 0:HSIZE] = (dot_nn(score, k_b[...]) * INV_ROOT).astype(BF16)
        dk_acc[...] += dot_tn(score, q_tile)
        op_part[rows, :] = dot_nn(att[rows, :], wo[...]).astype(BF16)
        rs_op.copy(d).start()

    rs_op = Scatter(p, op_part, near.at[1], made.at[1], land.at[1], rs_send.at[1], rs_recv.at[1])
    ag_cot.arrive(6, 7)
    attend(3)
    ag_cot.arrive(8)
    attend(1)
    ag_cot.share_far()
    attend(0)
    rs_op.direct()
    ag_cot.arrive(9)
    attend(2)
    ag_x.finish()
    dcat[:, HSIZE : 2 * HSIZE] = (dk_acc[...] * INV_ROOT).astype(BF16)
    dcat[:, 2 * HSIZE :] = dv_acc[...].astype(BF16)

    gn_part = xall
    rs_gn = Scatter(p, gn_part, near.at[0], made.at[0], land.at[0], rs_send.at[0], rs_recv.at[0])
    for d in (2, 1, 3, 0):
        rows = pl.ds(pair_rows(d), 256)
        gn_part[rows, :] = dot_nn(dcat[rows, :], wqkv[...]).astype(BF16)
        rs_gn.copy(d).start()
    rs_gn.far()
    rs_gn.direct()
    grad1, grad2, grad3 = red1[0], red2[0], red3[0]

    @pl.loop(0, 4)
    def _(i):
        columns = pl.ds(pl.multiple_of(i * 384, 384), 384)
        value = dot_tn(normed[:, columns], dcat[...]).astype(BF16)
        grad1[pl.ds(2 * i, 2), :, :, :, 0:576] = value.reshape(2, 2, 2, 48, 576)
        value = (dot_tn(cotall[:, columns], att[...]) * inv_tokens).astype(BF16)
        grad1[pl.ds(2 * i, 2), :, :, :, 576:768] = value.reshape(2, 2, 2, 48, HSIZE)

    rd1.begin()
    rs_gn.second()
    rs_gn.total(rows_f32)

    own = pl.multiple_of(mine * ROWS, ROWS)

    @pl.loop(0, 4)
    def _(i):
        rows = pl.ds(pl.multiple_of(i * 32, 32), 32)
        total = rows_f32[rows, :]
        wide = resid[rows, :].astype(F32)
        scale = rms_scale(wide)
        gr[pl.ds(own + i * 32, 32), :] = (
            cotall[pl.ds(own + i * 32, 32), :].astype(F32) * inv_tokens
            + scale * total
            - wide * scale**3 * jnp.mean(total * wide, axis=-1, keepdims=True)
        ).astype(BF16)

    gm_value = dot_nt(gr[pl.ds(own, ROWS), :], pwall[...]).astype(BF16)
    for j in range(8):
        gms[j, :, :] = gm_value[:, j * 128 : (j + 1) * 128]
    spots = [(d, side) for d in (2, 1, 3, 0) for side in (0, 1) if (d, side) != (0, 0)]

    def gm_copy(k):
        block, device = spot(p, *spots[k])
        return remote(gms.at[block], gmr.at[pl.ds(own, ROWS)], gm_send.at[k], gm_recv.at[k], device)

    def gm_arrive(k):
        d, side = spots[k]
        block, device = spot(p, (4 - d) % 4, side)
        here = gmr.at[pl.ds(pl.multiple_of(block * ROWS, ROWS), ROWS)]
        remote(gms.at[0], here, gm_send.at[k], gm_recv.at[k], device).wait_recv()

    for k in range(7):
        gm_copy(k).start()
    ag_gr.begin()
    gmr[pl.ds(own, ROWS), :] = gms[mine]
    rd1.second()
    for k in range(7):
        gm_arrive(k)

    @pl.loop(0, 8)
    def _(i):
        rows = pl.ds(pl.multiple_of(i * 128, 128), 128)
        value = gelu_back(cpre[rows, :], gmr[rows, :].astype(F32))
        gpad[pl.ds(pl.multiple_of(i * 128 + STEP, STEP), 128), :] = value.astype(BF16)

    moved[:, 0:INNER] = gpad[2 * STEP :, 0:INNER]
    moved[:, INNER : 2 * INNER] = gpad[STEP : LEN + STEP, 0:INNER]
    moved[:, 2 * INNER :] = gpad[0:LEN, 0:INNER]

    @pl.loop(0, 4)
    def _(i):
        columns = pl.ds(pl.multiple_of(i * 384, 384), 384)
        value = dot_tn(act[:, columns], moved[...]).astype(BF16)
        grad2[pl.ds(2 * i, 2)] = value[:, 0:256].reshape(2, 2, 2, 48, 256)
        grad3[pl.ds(2 * i, 2), :, :, :, INNER:128] = value[:, 256:].reshape(2, 2, 2, 48, 32)

    rd2.begin()
    ag_gr.forward()
    rs_op.far()
    ag_gr.share()
    rd1.third()
    ag_gr.share_far()
    rd2.second()
    ag_gr.arrive(6, 7, 8, 9)

    @pl.loop(0, 4)
    def _(i):
        columns = pl.ds(pl.multiple_of(i * 384, 384), 384)
        value = dot_tn(gr[:, columns], mid[...]).astype(BF16)
        grad3[pl.ds(2 * i, 2), :, :, :, 0:INNER] = value[:, 0:INNER].reshape(2, 2, 2, 48, INNER)

    rd3.begin()
    rd2.third()
    rs_op.second()
    rd3.second()
    rd3.third()
    rs_op.total(rows_f32)
    out_low[...] = (resid[...].astype(F32) + rows_f32[...]).astype(BF16)
    home = remote(out_low, out_home, home_send, home_recv, p.swap)
    home.start()
    rd1.fourth()
    rd2.fourth()
    rd3.fourth()
    for rd in (rd1, rd2, rd3):
        rd.finish()
    home.wait_recv()
    home.wait_send()
    swap_copy(0).wait_send()
    swap_copy(2).wait_send()

    @pl.when(crossed)
    def _():
        swap_copy(1).wait_send()
        for k in range(7):
            piece_sent(k).wait_send()
            piece_half(k, 1, p.xl, rd1.near).wait_send()

    for k in range(7):
        gm_copy(k).wait_send()
    for part in (rs_gn, rs_op, ag_pw, ag_mid, ag_cot, ag_gr):
        part.finish()


def shape(*dims, dtype=BF16):
    return jax.ShapeDtypeStruct(dims, dtype)


def reduce_scratch(width):
    half = pltpu.VMEM((4, 2, 48, width), BF16)
    part = pltpu.VMEM((4, 48, width), BF16)
    return (
        pltpu.VMEM((8, 2, 2, 48, width), BF16), half, half, part, part, part, part,
        pltpu.VMEM((8, 48, width), BF16), pltpu.VMEM((7, 48, width), BF16), pltpu.VMEM((48, width), BF16),
    )


def layer(inv_tokens, x, dil, pw, cot, wq, wk, wv, wo):
    whole = pltpu.VMEM((LEN, CH), BF16)
    head = pltpu.VMEM((LEN, HSIZE), BF16)
    dma = pltpu.SemaphoreType.DMA
    return pl.pallas_call(
        functools.partial(layer_kernel, inv_tokens),
        name="layer",
        out_shape=(shape(ROWS, CH), shape(48, 768), shape(48, 256), shape(48, 128)),
        in_specs=[ANY_SPEC] * 8,
        out_specs=(VMEM_SPEC,) * 4,
        scratch_shapes=[
            whole, whole,
            pltpu.VMEM((LEN + 2 * STEP, 384), F32),
            pltpu.VMEM((LEN, 128), F32),
            pltpu.VMEM((LEN, 128), BF16),
            pltpu.VMEM((LEN, 1024), BF16),
            pltpu.VMEM((1024, CH), BF16),
            whole, whole,
            pltpu.VMEM((384, CH), BF16),
            pltpu.VMEM((3 * HSIZE, CH), BF16),
            pltpu.VMEM((HSIZE, CH), BF16),
            pltpu.VMEM((ROWS, CH), BF16),
            whole,
            head, head, head, head,
            pltpu.VMEM((LEN, 3 * HSIZE), BF16),
            pltpu.VMEM((LEN, HSIZE), F32),
            pltpu.VMEM((LEN, HSIZE), F32),
            whole,
            pltpu.VMEM((8, 128, 128), BF16),
            pltpu.VMEM((LEN, 128), BF16),
            pltpu.VMEM((LEN + 2 * STEP, 128), BF16),
            pltpu.VMEM((LEN, 3 * INNER), BF16),
            pltpu.VMEM((ROWS, CH), F32),
            pltpu.VMEM((ROWS, CH), BF16),
            pltpu.VMEM((2, 4, ROWS, CH), BF16),
            pltpu.VMEM((2, 6, 64, CH), BF16),
            pltpu.VMEM((2, 6, 64, CH), BF16),
            reduce_scratch(768),
            reduce_scratch(256),
            reduce_scratch(128),
            dma((3,)), dma((3,)), dma((2, 7)), dma((2, 7)), dma((8,)), dma((5, 10)), dma((5, 10)), dma((2, 10)), dma((2, 10)),
            dma((3, 14)), dma((3, 14)), dma((7,)), dma((7,)), dma, dma,
        ],
        compiler_params=pltpu.CompilerParams(
            collective_id=0, has_side_effects=True, vmem_limit_bytes=LIMIT
        ),
    )(x, dil, pw, cot, wq, wk, wv, wo)


def split_kernel(low, h1, h2, h3, output, gd, gp, gq, gk, gv, go):
    output[0] = low[...]
    wide = h1[...].astype(F32)
    gq[...] = wide[:, 0:HSIZE]
    gk[...] = wide[:, HSIZE : 2 * HSIZE]
    gv[...] = wide[:, 2 * HSIZE : 3 * HSIZE]
    go[...] = wide[:, 3 * HSIZE :]
    taps = h2[...].astype(F32)
    rest = h3[...].astype(F32)
    gd[0] = taps[:, 0:INNER]
    gd[1] = taps[:, INNER : 2 * INNER]
    gd[2, :, 0:64] = taps[:, 2 * INNER :]
    gd[2, :, 64:INNER] = rest[:, INNER:]
    gp[...] = rest[:, 0:INNER]


def shards(x, dil, pw, wq, wk, wv, wo, cot):
    inv_tokens = 1.0 / math.sqrt(BATCH * LEN)
    homes = layer(inv_tokens, x, dil, pw, cot, wq, wk, wv, wo)
    square = shape(48, HSIZE, dtype=F32)
    output, gd, gp, gq, gk, gv, go = pl.pallas_call(
        split_kernel,
        name="split",
        out_shape=(
            shape(1, ROWS, CH), shape(3, 48, INNER, dtype=F32), shape(48, INNER, dtype=F32),
            square, square, square, square,
        ),
        in_specs=[VMEM_SPEC] * 4,
        out_specs=(VMEM_SPEC,) * 7,
    )(*homes)
    return (output, gd, gp.T, gq, gk, gv, go.T)


def solution(mesh):
    torus = Mesh(mesh.devices.reshape(8, 2, 2, 4, 2), AXES)
    in_specs = (
        P(DP, SEQ, None),
        P(None, SEQ, None),
        P(SEQ, None),
        P(SEQ, None),
        P(SEQ, None),
        P(SEQ, None),
        P(SEQ, None),
        P(DP, SEQ, None),
    )
    out_specs = (
        P(DP, SEQ, None),
        P(None, DP, SEQ),
        P(SEQ, DP),
        P(DP, SEQ),
        P(DP, SEQ),
        P(DP, SEQ),
        P(SEQ, DP),
    )
    return jax.shard_map(
        shards, mesh=torus, in_specs=in_specs, out_specs=out_specs, check_vma=False
    )
```

```python
import functools
import math

import jax
import jax.numpy as jnp
from jax import lax
from jax.experimental import pallas as pl
from jax.experimental.pallas import tpu as pltpu
from jax.sharding import Mesh
from jax.sharding import PartitionSpec as P

HSIZE = 192
STEP = 16
EPSILON = 1e-06
SOFT_CAP = 6.0
LEN = 1024
CH = 1536
INNER = 96
ROWS = 128
BATCH = 32
AXES = ("z", "xl", "c", "y", "xh")
DP = ("z", "xl", "c")
SEQ = ("y", "xh")
MESH_ID = pl.DeviceIdType.MESH
F32 = jnp.float32
BF16 = jnp.bfloat16
VMEM_SPEC = pl.BlockSpec(memory_space=pltpu.VMEM)
ANY_SPEC = pl.BlockSpec(memory_space=pl.ANY)
LIMIT = 62 * 1024 * 1024


def dot_nt(a, b):
    return lax.dot_general(a, b, (((1,), (1,)), ((), ())), preferred_element_type=F32)


def dot_nn(a, b):
    return jnp.dot(a, b, preferred_element_type=F32)


def dot_tn(a, b):
    return lax.dot_general(a, b, (((0,), (0,)), ((), ())), preferred_element_type=F32)


def rms_scale(rows):
    return lax.rsqrt(jnp.mean(rows * rows, axis=-1, keepdims=True) + EPSILON)


def gelu_back(pre_act, upstream):
    return jax.vjp(jax.nn.gelu, pre_act)[1](upstream)[0]


class Place:
    def __init__(self):
        self.z = lax.axis_index("z")
        self.xl = lax.axis_index("xl")
        self.c = lax.axis_index("c")
        self.y = lax.axis_index("y")
        self.xh = lax.axis_index("xh")
        self.up = {"y": lax.rem(self.y + 1, 4)}
        self.down = {"y": lax.rem(self.y + 3, 4)}
        self.twin = {"c": 1 - self.c}
        self.swap = {"xl": 1 - self.xl, "xh": self.c, "c": self.xh}

    def block(self, d, mine=True):
        return lax.rem(self.y + d, 4) * 2 + (self.c if mine else 1 - self.c)


def greet(devices):
    barrier = pltpu.get_barrier_semaphore()
    for device in devices:
        pl.semaphore_signal(barrier, inc=1, device_id=device, device_id_type=MESH_ID)
    pl.semaphore_wait(barrier, len(devices))


def remote(src, dst, send, recv, device):
    return pltpu.make_async_remote_copy(
        src_ref=src, dst_ref=dst, send_sem=send, recv_sem=recv,
        device_id=device, device_id_type=MESH_ID,
    )


class Gather:
    def __init__(self, place, view, send, recv):
        self.view, self.send, self.recv = view, send, recv
        p = place
        own, low, high, far = (p.block(d) for d in (0, 3, 1, 2))
        own2, low2, high2, far2 = (p.block(d, False) for d in (0, 3, 1, 2))
        self.out = [
            (own, 0, p.up), (own, 1, p.up), (low, 0, p.up),
            (own, 1, p.down), (own, 0, p.down), (high, 1, p.down),
            (own, None, p.twin), (low, None, p.twin), (high, None, p.twin), (far, None, p.twin),
        ]
        self.inn = [
            (low, 0), (low, 1), (far, 0), (high, 1), (high, 0), (far, 1),
            (own2, None), (low2, None), (high2, None), (far2, None),
        ]

    def copy(self, k):
        block, half, device = self.out[k]
        ref = self.view(block, half)
        return remote(ref, ref, self.send.at[k], self.recv.at[k], device)

    def start(self, *ks):
        for k in ks:
            self.copy(k).start()

    def arrive(self, *ks):
        for k in ks:
            block, half = self.inn[k]
            ref = self.view(block, half)
            remote(ref, ref, self.send.at[k], self.recv.at[k], self.out[k][2]).wait_recv()

    def begin(self):
        self.start(0, 3, 1, 4, 6)

    def forward(self):
        self.arrive(0)
        self.start(2)
        self.arrive(3)
        self.start(5)

    def share(self):
        self.arrive(1)
        self.start(7)
        self.arrive(4)
        self.start(8)

    def share_far(self):
        self.arrive(2, 5)
        self.start(9)

    def finish(self):
        for k in range(10):
            self.copy(k).wait_send()


def row_view(ref, pitch, rows):
    def view(block, half):
        if half is None:
            return ref.at[pl.ds(pl.multiple_of(block * pitch, pitch), rows)]
        start = pl.multiple_of(block * pitch + half * (rows // 2), 16)
        return ref.at[pl.ds(start, rows // 2)]
    return view


def column_view(ref):
    def view(block, half):
        columns = pl.ds(pl.multiple_of(block * 128, 128), 128)
        if half is None:
            return ref.at[:, columns]
        return ref.at[pl.ds(half * (LEN // 2), LEN // 2), columns]
    return view


def spot(p, d, side):
    core = p.c if side == 0 else 1 - p.c
    y = lax.rem(p.y + d, 4)
    return y * 2 + core, ({"y": y} if side == 0 else {"y": y, "c": core})


class Scatter:
    def __init__(self, place, part, near, made, land, send, recv):
        self.p, self.part, self.near, self.made, self.land = place, part, near, made, land
        self.send, self.recv = send, recv

    def own_rows(self, d, half):
        start = pl.multiple_of(self.p.block(d) * ROWS + half * 64, 64)
        return self.part[pl.ds(start, 64), :].astype(F32)

    def both(self, d, half):
        rows = slice(half * 64, half * 64 + 64)
        return self.own_rows(d, half) + self.near[d, rows, :].astype(F32)

    def copies(self, k):
        p = self.p
        if k < 4:
            start = pl.multiple_of(p.block(k, False) * ROWS, ROWS)
            return self.part.at[pl.ds(start, ROWS)], self.near.at[k], p.twin
        d, half, device = [
            (2, 0, p.down), (2, 1, p.up), (1, 0, p.up), (3, 1, p.down), (3, 0, p.down), (1, 1, p.up)
        ][k - 4]
        return self.made.at[k - 4], self.land.at[k - 4], device

    def copy(self, k):
        src, dst, device = self.copies(k)
        return remote(src, dst, self.send.at[k], self.recv.at[k], device)

    def begin(self):
        for d in (2, 1, 3, 0):
            self.copy(d).start()

    def make(self, k, value):
        self.made[k - 4, :, :] = value.astype(BF16)
        self.copy(k).start()

    def direct(self):
        self.copy(1).wait_recv()
        self.make(6, self.both(1, 0))
        self.copy(3).wait_recv()
        self.make(7, self.both(3, 1))

    def far(self):
        self.copy(2).wait_recv()
        self.make(4, self.both(2, 0))
        self.make(5, self.both(2, 1))

    def second(self):
        self.copy(4).wait_recv()
        self.make(8, self.both(3, 0) + self.land[0].astype(F32))
        self.copy(5).wait_recv()
        self.make(9, self.both(1, 1) + self.land[1].astype(F32))

    def total(self, out):
        self.copy(0).wait_recv()
        for k in (6, 7, 8, 9):
            self.copy(k).wait_recv()
        out[0:64, :] = self.both(0, 0) + self.land[2].astype(F32) + self.land[4].astype(F32)
        out[64:128, :] = self.both(0, 1) + self.land[3].astype(F32) + self.land[5].astype(F32)

    def finish(self):
        for k in range(10):
            self.copy(k).wait_send()


class Reduce:
    def __init__(self, place, grad, r1a, r1b, sa, sb, r2a, r2b, quarter, landed, final, home, send, recv):
        self.p, self.grad = place, grad
        self.r1a, self.r1b, self.sa, self.sb, self.r2a, self.r2b = r1a, r1b, sa, sb, r2a, r2b
        self.quarter, self.landed, self.final, self.home = quarter, landed, final, home
        self.send, self.recv = send, recv
        p = place
        self.near = {"xl": 1 - p.xl}
        self.cross = {"xl": 1 - p.xl, "xh": 1 - p.xh}
        odd = lax.rem(p.xl + p.xh, 2)
        self.keep = [lax.rem(odd + 1 - k, 2) for k in range(2)]

    def copy(self, k):
        p = self.p
        if k < 2:
            src, dst, device = self.grad.at[pl.ds(0, 4), k, 1 - self.keep[k]], self.r1a.at[:, k], self.near
        elif k < 4:
            src, dst, device = self.grad.at[pl.ds(4, 4), k - 2, 1 - p.xh], self.r1b.at[:, k - 2], self.cross
        elif k == 4:
            src, dst, device = self.sa, self.r2a, self.cross
        elif k == 5:
            src, dst, device = self.sb, self.r2b, self.near
        elif k < 13:
            dz = k - 5
            target = lax.rem(p.z + dz, 8)
            src, dst, device = self.quarter.at[target], self.landed.at[dz - 1], {"z": target}
        else:
            src, dst, device = self.final, self.home, p.swap
        return remote(src, dst, self.send.at[k], self.recv.at[k], device)

    def begin(self):
        for k in range(4):
            self.copy(k).start()

    def second(self):
        p = self.p
        for k in range(4):
            self.copy(k).wait_recv()
        keep = [self.grad[0:4, k, self.keep[k]].astype(F32) + self.r1a[:, k].astype(F32) for k in range(2)]
        mine = p.xl == 0
        self.sa[...] = jnp.where(mine, keep[0], keep[1]).astype(BF16)
        self.copy(4).start()
        self.quarter[0:4] = jnp.where(mine, keep[1], keep[0]).astype(BF16)
        keep = [self.grad[4:8, k, p.xh].astype(F32) + self.r1b[:, k].astype(F32) for k in range(2)]
        self.sb[...] = jnp.where(mine, keep[0], keep[1]).astype(BF16)
        self.copy(5).start()
        self.quarter[4:8] = jnp.where(mine, keep[1], keep[0]).astype(BF16)

    def third(self):
        self.copy(4).wait_recv()
        self.quarter[0:4] = (self.quarter[0:4].astype(F32) + self.r2a[...].astype(F32)).astype(BF16)
        self.copy(5).wait_recv()
        self.quarter[4:8] = (self.quarter[4:8].astype(F32) + self.r2b[...].astype(F32)).astype(BF16)
        for dz in (4, 3, 5, 2, 6, 1, 7):
            self.copy(5 + dz).start()

    def fourth(self):
        total = self.quarter[self.p.z].astype(F32)
        for dz in range(1, 8):
            self.copy(5 + dz).wait_recv()
            total = total + self.landed[dz - 1].astype(F32)
        self.final[...] = total.astype(BF16)
        self.copy(13).start()

    def finish(self):
        self.copy(13).wait_recv()
        for k in range(14):
            self.copy(k).wait_send()


class Wide:
    def __init__(self, place, grad, landed, total, slots, final, home, send, recv):
        self.p, self.grad, self.landed, self.total = place, grad, landed, total
        self.slots, self.final, self.home, self.send, self.recv = slots, final, home, send, recv

    def copy(self, k):
        p = self.p
        if k < 7:
            target = lax.rem(p.z + k + 1, 8)
            src, dst, device = self.grad.at[target], self.landed.at[k], {"z": target}
        elif k == 7:
            src, dst, device = self.total.at[p.xl, p.xh], self.slots.at[0], {"xl": 1 - p.xl}
        elif k == 8:
            src, dst = self.total.at[p.xl, 1 - p.xh], self.slots.at[1]
            device = {"xl": 1 - p.xl, "xh": 1 - p.xh}
        elif k == 9:
            src, dst, device = self.total.at[1 - p.xl, 1 - p.xh], self.slots.at[2], {"xh": 1 - p.xh}
        else:
            src, dst, device = self.final, self.home, p.swap
        return remote(src, dst, self.send.at[k], self.recv.at[k], device)

    def begin(self):
        for dz in (4, 3, 5, 2, 6, 1, 7):
            self.copy(dz - 1).start()

    def second(self):
        total = self.grad[self.p.z].astype(F32)
        for k in range(7):
            self.copy(k).wait_recv()
            total = total + self.landed[k].astype(F32)
        self.total[...] = total.astype(BF16)
        for k in (7, 8, 9):
            self.copy(k).start()

    def third(self):
        total = self.total[1 - self.p.xl, self.p.xh].astype(F32)
        for k in (7, 8, 9):
            self.copy(k).wait_recv()
            total = total + self.slots[k - 7].astype(F32)
        self.final[...] = total.astype(BF16)
        self.copy(10).start()

    def finish(self):
        self.copy(10).wait_recv()
        for k in range(11):
            self.copy(k).wait_send()


INV_ROOT = 1.0 / math.sqrt(HSIZE)


def layer_kernel(
    inv_tokens,
    x_ref, dil_ref, pw_ref, cot_ref, wq_ref, wk_ref, wv_ref, wo_ref,
    out_home, home1, home2, home3, home4,
    xall, act, taps, cpre, mid, midall, pwall, cotall, normed, dil, wqkv, wo, resid, op_part,
    q_b, k_b, v_b, att, dcat, dk_acc, dv_acc, gr, gms, gmr, gpad, moved, rows_f32, out_low,
    near, made, land, red1, red2, red3, red4,
    swap_send, swap_recv, piece_send, piece_recv, local_sem, ag_send, ag_recv, rs_send, rs_recv, rd_send, rd_recv, wd_send, wd_recv, gm_send, gm_recv, home_send, home_recv,
):
    p = Place()
    mine = p.block(0)
    there = p.y * 2 + p.xh
    taps[0:STEP, :] = jnp.zeros((STEP, 384), F32)
    taps[LEN + STEP :, :] = jnp.zeros((STEP, 384), F32)
    gpad[0:STEP, :] = jnp.zeros((STEP, 128), BF16)
    gpad[LEN + STEP :, :] = jnp.zeros((STEP, 128), BF16)
    for j in range(8):
        pwall[j * 128 + INNER : (j + 1) * 128, :] = jnp.zeros((32, CH), BF16)
    for k in range(3):
        dil[k * 128 + INNER : (k + 1) * 128, :] = jnp.zeros((32, CH), BF16)

    rd1 = Reduce(p, *red1, home1, rd_send.at[0], rd_recv.at[0])
    rd2 = Reduce(p, *red2, home2, rd_send.at[1], rd_recv.at[1])
    rd3 = Reduce(p, *red3, home3, rd_send.at[2], rd_recv.at[2])
    early = Wide(p, *red4, home4, wd_send, wd_recv)
    greet(
        [p.swap, rd1.near, rd1.cross, {"xh": 1 - p.xh}, p.twin]
        + [spot(p, d, side)[1] for d in (1, 2, 3) for side in (0, 1)]
        + [{"z": lax.rem(p.z + dz, 8)} for dz in range(1, 8)]
    )

    def at(ref, block, pitch, rows):
        return ref.at[pl.ds(pl.multiple_of(block * pitch, pitch), rows)]

    def piece(ref, k, rows):
        return ref.at[pl.ds(k, rows)]

    swaps = [
        (x_ref.at[0], at(xall, there, ROWS, ROWS), at(xall, mine, ROWS, ROWS)),
        (pw_ref, at(pwall, there, 128, INNER), at(pwall, mine, 128, INNER)),
        (cot_ref.at[0], at(cotall, there, ROWS, ROWS), at(cotall, mine, ROWS, ROWS)),
    ]
    crossed = p.c != p.xh

    def swap_copy(k):
        src, dst, _ = swaps[k]
        return remote(src, dst, swap_send.at[k], swap_recv.at[k], p.swap)

    def swap_arrive(k):
        src, _, here = swaps[k]
        remote(src, here, swap_send.at[k], swap_recv.at[k], p.swap).wait_recv()

    pieces = [
        *[(dil_ref.at[k], dil, k * 128, INNER) for k in range(3)],
        *[(ref, wqkv, k * HSIZE, HSIZE) for k, ref in enumerate((wq_ref, wk_ref, wv_ref))],
        (wo_ref, wo, 0, HSIZE),
    ]

    def part_of(ref, base, rows, half):
        return ref.at[pl.ds(pl.multiple_of(base + half * (rows // 2), 16), rows // 2)]

    def piece_sent(k):
        src, dst, base, rows = pieces[k]
        half = 1 - p.xl
        return remote(part_of(src, 0, rows, half), part_of(dst, base, rows, half),
                      piece_send.at[0, k], piece_recv.at[0, k], p.swap)

    def piece_half(k, stage, half, device):
        _, dst, base, rows = pieces[k]
        ref = part_of(dst, base, rows, half)
        return remote(ref, ref, piece_send.at[stage, k], piece_recv.at[stage, k], device)

    def piece_local(k):
        src, dst, base, rows = pieces[k]
        return pltpu.make_async_copy(src, piece(dst, base, rows), local_sem.at[k])

    def piece_pass(*ks):
        @pl.when(crossed)
        def _():
            for k in ks:
                piece_half(k, 0, p.xl, p.swap).wait_recv()
                piece_half(k, 1, p.xl, rd1.near).start()

    def piece_arrive(*ks):
        @pl.when(crossed)
        def _():
            for k in ks:
                piece_half(k, 1, 1 - p.xl, rd1.near).wait_recv()

        @pl.when(jnp.logical_not(crossed))
        def _():
            for k in ks:
                piece_local(k).wait()

    pw_local = pltpu.make_async_copy(pw_ref, at(pwall, mine, 128, INNER), local_sem.at[7])

    ag_x = Gather(p, row_view(xall, ROWS, ROWS), ag_send.at[0], ag_recv.at[0])
    ag_pw = Gather(p, row_view(pwall, 128, INNER), ag_send.at[1], ag_recv.at[1])
    ag_mid = Gather(p, column_view(midall), ag_send.at[2], ag_recv.at[2])
    ag_cot = Gather(p, row_view(cotall, ROWS, ROWS), ag_send.at[3], ag_recv.at[3])
    ag_gr = Gather(p, row_view(gr, ROWS, ROWS), ag_send.at[4], ag_recv.at[4])

    def pair_rows(d):
        return pl.multiple_of(lax.rem(p.y + d, 4) * 256, 256)

    def activate(d):
        base = pair_rows(d)

        @pl.loop(0, 8)
        def _(i):
            rows = pl.ds(pl.multiple_of(base + i * 32, 32), 32)
            value = xall[rows, :].astype(F32)
            act[rows, :] = jax.nn.gelu(value * rms_scale(value)).astype(BF16)

    def tap(d):
        base = pair_rows(d)
        taps[pl.ds(base + STEP, 256), :] = dot_nt(act[pl.ds(base, 256), :], dil[...])

    swap_copy(0).start()

    @pl.when(crossed)
    def _():
        for k in range(3):
            piece_sent(k).start()
        swap_copy(1).start()

    swap_copy(2).start()

    @pl.when(crossed)
    def _():
        for k in range(3, 7):
            piece_sent(k).start()

    @pl.when(jnp.logical_not(crossed))
    def _():
        pw_local.start()
        for k in range(7):
            piece_local(k).start()
        pw_local.wait()
        ag_pw.begin()
        ag_pw.forward()

    swap_arrive(0)
    ag_x.begin()
    ag_x.arrive(6)
    activate(0)
    ag_x.forward()
    piece_pass(0, 1, 2)
    ag_x.share()
    piece_arrive(0, 1, 2)
    tap(0)
    ag_x.arrive(7)
    activate(3)
    tap(3)
    ag_x.share_far()

    @pl.when(crossed)
    def _():
        swap_arrive(1)
        ag_pw.begin()

    ag_x.arrive(8)
    activate(1)
    tap(1)

    @pl.when(crossed)
    def _():
        ag_pw.forward()

    ag_x.arrive(9)
    activate(2)
    tap(2)

    @pl.loop(0, 8)
    def _(i):
        base = pl.multiple_of(i * 128, 128)
        total = (
            taps[pl.ds(base, 128), 0:128]
            + taps[pl.ds(base + STEP, 128), 128:256]
            + taps[pl.ds(base + 2 * STEP, 128), 256:384]
        )
        cpre[pl.ds(base, 128), :] = total
        low = jax.nn.gelu(total).astype(BF16)
        mid[pl.ds(base, 128), :] = low
        midall[pl.ds(base, 128), pl.ds(pl.multiple_of(mine * 128, 128), 128)] = low

    ag_mid.begin()
    ag_pw.share()
    ag_pw.share_far()
    ag_mid.forward()
    swap_arrive(2)
    ag_cot.begin()
    piece_pass(3, 4, 5, 6)
    ag_mid.share()
    ag_mid.share_far()
    ag_pw.arrive(6, 7, 8, 9)
    ag_mid.arrive(6, 7, 8, 9)

    @pl.loop(0, 4)
    def _(i):
        rows = pl.ds(pl.multiple_of(i * 256, 256), 256)
        total = xall[rows, :].astype(F32) + dot_nn(midall[rows, :], pwall[...])
        low = total.astype(BF16)
        wide = low.astype(F32)
        normed[rows, :] = (wide * rms_scale(wide)).astype(BF16)

        @pl.when(i == p.y)
        def _():
            resid[...] = jnp.where(p.c == 0, low[0:128], low[128:256])

    ag_cot.forward()
    piece_arrive(3, 4, 5)

    @pl.loop(0, 4)
    def _(i):
        rows = pl.ds(pl.multiple_of(i * 256, 256), 256)
        tile = normed[rows, :]
        q_b[rows, :] = dot_nt(tile, wqkv[0:HSIZE, :]).astype(BF16)
        k_b[rows, :] = dot_nt(tile, wqkv[HSIZE : 2 * HSIZE, :]).astype(BF16)
        v_b[rows, :] = dot_nt(tile, wqkv[2 * HSIZE :, :]).astype(BF16)

    ag_cot.share()
    piece_arrive(6)
    dk_acc[...] = jnp.zeros_like(dk_acc)
    dv_acc[...] = jnp.zeros_like(dv_acc)

    def attend(d):
        rows = pl.ds(pair_rows(d), 256)
        gh_tile = (dot_nt(cotall[rows, :], wo[...]) * inv_tokens).astype(BF16)
        q_tile = q_b[rows, :]
        ratio = jnp.tanh(dot_nt(q_tile, k_b[...]) * (INV_ROOT / SOFT_CAP))
        unnormed = jnp.exp(SOFT_CAP * ratio)
        weights = unnormed * (1.0 / jnp.sum(unnormed, axis=-1, keepdims=True))
        weights_low = weights.astype(BF16)
        attended = dot_nn(weights_low, v_b[...])
        att[rows, :] = attended.astype(BF16)
        dv_acc[...] += dot_tn(weights_low, gh_tile)
        grad_soft = dot_nt(gh_tile, v_b[...])
        mean_grad = jnp.sum(gh_tile.astype(F32) * attended, axis=-1, keepdims=True)
        grad_capped = weights * (grad_soft - mean_grad)
        score = (grad_capped * (1.0 - ratio * ratio)).astype(BF16)
        dcat[rows, 0:HSIZE] = (dot_nn(score, k_b[...]) * INV_ROOT).astype(BF16)
        dk_acc[...] += dot_tn(score, q_tile)
        op_part[rows, :] = dot_nn(att[rows, :], wo[...]).astype(BF16)
        rs_op.copy(d).start()

    rs_op = Scatter(p, op_part, near.at[1], made.at[1], land.at[1], rs_send.at[1], rs_recv.at[1])
    ag_cot.arrive(6, 7)
    attend(3)
    ag_cot.arrive(8)
    attend(1)
    ag_cot.share_far()
    attend(0)
    rs_op.direct()
    ag_cot.arrive(9)
    attend(2)
    ag_x.finish()
    dcat[:, HSIZE : 2 * HSIZE] = (dk_acc[...] * INV_ROOT).astype(BF16)
    dcat[:, 2 * HSIZE :] = dv_acc[...].astype(BF16)

    gn_part = xall
    rs_gn = Scatter(p, gn_part, near.at[0], made.at[0], land.at[0], rs_send.at[0], rs_recv.at[0])
    for d in (2, 1, 3, 0):
        rows = pl.ds(pair_rows(d), 256)
        gn_part[rows, :] = dot_nn(dcat[rows, :], wqkv[...]).astype(BF16)
        rs_gn.copy(d).start()
    rs_gn.far()
    rs_gn.direct()
    grad1, grad2, grad3, grad4 = red1[0], red2[0], red3[0], red4[0]

    @pl.loop(0, 4)
    def _(i):
        columns = pl.ds(pl.multiple_of(i * 384, 384), 384)
        value = dot_tn(normed[:, columns], dcat[...]).astype(BF16)
        grad1[pl.ds(2 * i, 2)] = value[:, 0:512].reshape(2, 2, 2, 48, 512)
        grad4[pl.ds(2 * i, 2), :, :, :, HSIZE:256] = value[:, 512:].reshape(2, 2, 2, 48, 64)

    rd1.begin()

    @pl.loop(0, 4)
    def _(i):
        columns = pl.ds(pl.multiple_of(i * 384, 384), 384)
        value = (dot_tn(cotall[:, columns], att[...]) * inv_tokens).astype(BF16)
        grad4[pl.ds(2 * i, 2), :, :, :, 0:HSIZE] = value.reshape(2, 2, 2, 48, HSIZE)

    early.begin()
    rs_gn.second()
    rs_gn.total(rows_f32)

    own = pl.multiple_of(mine * ROWS, ROWS)

    @pl.loop(0, 4)
    def _(i):
        rows = pl.ds(pl.multiple_of(i * 32, 32), 32)
        total = rows_f32[rows, :]
        wide = resid[rows, :].astype(F32)
        scale = rms_scale(wide)
        gr[pl.ds(own + i * 32, 32), :] = (
            cotall[pl.ds(own + i * 32, 32), :].astype(F32) * inv_tokens
            + scale * total
            - wide * scale**3 * jnp.mean(total * wide, axis=-1, keepdims=True)
        ).astype(BF16)

    gm_value = dot_nt(gr[pl.ds(own, ROWS), :], pwall[...]).astype(BF16)
    for j in range(8):
        gms[j, :, :] = gm_value[:, j * 128 : (j + 1) * 128]
    spots = [(d, side) for d in (2, 1, 3, 0) for side in (0, 1) if (d, side) != (0, 0)]

    def gm_copy(k):
        block, device = spot(p, *spots[k])
        return remote(gms.at[block], gmr.at[pl.ds(own, ROWS)], gm_send.at[k], gm_recv.at[k], device)

    def gm_arrive(k):
        d, side = spots[k]
        block, device = spot(p, (4 - d) % 4, side)
        here = gmr.at[pl.ds(pl.multiple_of(block * ROWS, ROWS), ROWS)]
        remote(gms.at[0], here, gm_send.at[k], gm_recv.at[k], device).wait_recv()

    for k in range(7):
        gm_copy(k).start()
    ag_gr.begin()
    gmr[pl.ds(own, ROWS), :] = gms[mine]
    rd1.second()
    for k in range(7):
        gm_arrive(k)

    @pl.loop(0, 8)
    def _(i):
        rows = pl.ds(pl.multiple_of(i * 128, 128), 128)
        value = gelu_back(cpre[rows, :], gmr[rows, :].astype(F32))
        gpad[pl.ds(pl.multiple_of(i * 128 + STEP, STEP), 128), :] = value.astype(BF16)

    moved[:, 0:INNER] = gpad[2 * STEP :, 0:INNER]
    moved[:, INNER : 2 * INNER] = gpad[STEP : LEN + STEP, 0:INNER]
    moved[:, 2 * INNER :] = gpad[0:LEN, 0:INNER]

    @pl.loop(0, 4)
    def _(i):
        columns = pl.ds(pl.multiple_of(i * 384, 384), 384)
        value = dot_tn(act[:, columns], moved[...]).astype(BF16)
        grad2[pl.ds(2 * i, 2)] = value[:, 0:256].reshape(2, 2, 2, 48, 256)
        grad3[pl.ds(2 * i, 2), :, :, :, INNER:128] = value[:, 256:].reshape(2, 2, 2, 48, 32)

    rd2.begin()
    ag_gr.forward()
    rs_op.far()
    ag_gr.share()
    rd1.third()
    early.second()
    ag_gr.share_far()
    rd2.second()
    ag_gr.arrive(6, 7, 8, 9)

    @pl.loop(0, 4)
    def _(i):
        columns = pl.ds(pl.multiple_of(i * 384, 384), 384)
        value = dot_tn(gr[:, columns], mid[...]).astype(BF16)
        grad3[pl.ds(2 * i, 2), :, :, :, 0:INNER] = value[:, 0:INNER].reshape(2, 2, 2, 48, INNER)

    rd3.begin()
    rd2.third()
    early.third()
    rs_op.second()
    rd3.second()
    rd3.third()
    rs_op.total(rows_f32)
    out_low[...] = (resid[...].astype(F32) + rows_f32[...]).astype(BF16)
    home = remote(out_low, out_home, home_send, home_recv, p.swap)
    home.start()
    rd1.fourth()
    rd2.fourth()
    rd3.fourth()
    for rd in (rd1, rd2, rd3, early):
        rd.finish()
    home.wait_recv()
    home.wait_send()
    swap_copy(0).wait_send()
    swap_copy(2).wait_send()

    @pl.when(crossed)
    def _():
        swap_copy(1).wait_send()
        for k in range(7):
            piece_sent(k).wait_send()
            piece_half(k, 1, p.xl, rd1.near).wait_send()

    for k in range(7):
        gm_copy(k).wait_send()
    for part in (rs_gn, rs_op, ag_pw, ag_mid, ag_cot, ag_gr):
        part.finish()


def shape(*dims, dtype=BF16):
    return jax.ShapeDtypeStruct(dims, dtype)


def reduce_scratch(width):
    half = pltpu.VMEM((4, 2, 48, width), BF16)
    part = pltpu.VMEM((4, 48, width), BF16)
    return (
        pltpu.VMEM((8, 2, 2, 48, width), BF16), half, half, part, part, part, part,
        pltpu.VMEM((8, 48, width), BF16), pltpu.VMEM((7, 48, width), BF16), pltpu.VMEM((48, width), BF16),
    )


def layer(inv_tokens, x, dil, pw, cot, wq, wk, wv, wo):
    whole = pltpu.VMEM((LEN, CH), BF16)
    head = pltpu.VMEM((LEN, HSIZE), BF16)
    dma = pltpu.SemaphoreType.DMA
    return pl.pallas_call(
        functools.partial(layer_kernel, inv_tokens),
        name="layer",
        out_shape=(shape(ROWS, CH), shape(48, 512), shape(48, 256), shape(48, 128), shape(48, 256)),
        in_specs=[ANY_SPEC] * 8,
        out_specs=(VMEM_SPEC,) * 5,
        scratch_shapes=[
            whole, whole,
            pltpu.VMEM((LEN + 2 * STEP, 384), F32),
            pltpu.VMEM((LEN, 128), F32),
            pltpu.VMEM((LEN, 128), BF16),
            pltpu.VMEM((LEN, 1024), BF16),
            pltpu.VMEM((1024, CH), BF16),
            whole, whole,
            pltpu.VMEM((384, CH), BF16),
            pltpu.VMEM((3 * HSIZE, CH), BF16),
            pltpu.VMEM((HSIZE, CH), BF16),
            pltpu.VMEM((ROWS, CH), BF16),
            whole,
            head, head, head, head,
            pltpu.VMEM((LEN, 3 * HSIZE), BF16),
            pltpu.VMEM((LEN, HSIZE), F32),
            pltpu.VMEM((LEN, HSIZE), F32),
            whole,
            pltpu.VMEM((8, 128, 128), BF16),
            pltpu.VMEM((LEN, 128), BF16),
            pltpu.VMEM((LEN + 2 * STEP, 128), BF16),
            pltpu.VMEM((LEN, 3 * INNER), BF16),
            pltpu.VMEM((ROWS, CH), F32),
            pltpu.VMEM((ROWS, CH), BF16),
            pltpu.VMEM((2, 4, ROWS, CH), BF16),
            pltpu.VMEM((2, 6, 64, CH), BF16),
            pltpu.VMEM((2, 6, 64, CH), BF16),
            reduce_scratch(512),
            reduce_scratch(256),
            reduce_scratch(128),
            (
                pltpu.VMEM((8, 2, 2, 48, 256), BF16), pltpu.VMEM((7, 2, 2, 48, 256), BF16),
                pltpu.VMEM((2, 2, 48, 256), BF16), pltpu.VMEM((3, 48, 256), BF16), pltpu.VMEM((48, 256), BF16),
            ),
            dma((3,)), dma((3,)), dma((2, 7)), dma((2, 7)), dma((8,)), dma((5, 10)), dma((5, 10)), dma((2, 10)), dma((2, 10)),
            dma((3, 14)), dma((3, 14)), dma((11,)), dma((11,)), dma((7,)), dma((7,)), dma, dma,
        ],
        compiler_params=pltpu.CompilerParams(
            collective_id=0, has_side_effects=True, vmem_limit_bytes=LIMIT
        ),
    )(x, dil, pw, cot, wq, wk, wv, wo)


def split_kernel(low, h1, h2, h3, h4, output, gd, gp, gq, gk, gv, go):
    output[0] = low[...]
    wide = h1[...].astype(F32)
    gq[...] = wide[:, 0:HSIZE]
    gk[...] = wide[:, HSIZE : 2 * HSIZE]
    last = h4[...].astype(F32)
    gv[:, 0:128] = wide[:, 2 * HSIZE :]
    gv[:, 128:HSIZE] = last[:, HSIZE:]
    go[...] = last[:, 0:HSIZE]
    taps = h2[...].astype(F32)
    rest = h3[...].astype(F32)
    gd[0] = taps[:, 0:INNER]
    gd[1] = taps[:, INNER : 2 * INNER]
    gd[2, :, 0:64] = taps[:, 2 * INNER :]
    gd[2, :, 64:INNER] = rest[:, INNER:]
    gp[...] = rest[:, 0:INNER]


def shards(x, dil, pw, wq, wk, wv, wo, cot):
    inv_tokens = 1.0 / math.sqrt(BATCH * LEN)
    homes = layer(inv_tokens, x, dil, pw, cot, wq, wk, wv, wo)
    square = shape(48, HSIZE, dtype=F32)
    output, gd, gp, gq, gk, gv, go = pl.pallas_call(
        split_kernel,
        name="split",
        out_shape=(
            shape(1, ROWS, CH), shape(3, 48, INNER, dtype=F32), shape(48, INNER, dtype=F32),
            square, square, square, square,
        ),
        in_specs=[VMEM_SPEC] * 5,
        out_specs=(VMEM_SPEC,) * 7,
    )(*homes)
    return (output, gd, gp.T, gq, gk, gv, go.T)


def solution(mesh):
    torus = Mesh(mesh.devices.reshape(8, 2, 2, 4, 2), AXES)
    in_specs = (
        P(DP, SEQ, None),
        P(None, SEQ, None),
        P(SEQ, None),
        P(SEQ, None),
        P(SEQ, None),
        P(SEQ, None),
        P(SEQ, None),
        P(DP, SEQ, None),
    )
    out_specs = (
        P(DP, SEQ, None),
        P(None, DP, SEQ),
        P(SEQ, DP),
        P(DP, SEQ),
        P(DP, SEQ),
        P(DP, SEQ),
        P(SEQ, DP),
    )
    return jax.shard_map(
        shards, mesh=torus, in_specs=in_specs, out_specs=out_specs, check_vma=False
    )
```
